512 devices in a mesh: span: 4 (over x), seq: 32 (over z_hi, y, core), head: 4 (over z_lo).
Axes of the slice: x: 4, y: 8, z: 8 (z_hi: 2, z_lo: 4; z = z_hi * 4 + z_lo), core: 2. Of those that a mesh axis runs over, the one named last changes fastest.
Arguments:
- query_proj: bfloat16 [4, 1280, 3072], P('span', 'seq', 'head'), may hold values from -12 to 12
- key_proj: bfloat16 [4, 1280, 3072], P('span', 'seq', 'head'), may hold values from -12 to 12
- value_proj: bfloat16 [4, 1280, 3072], P('span', 'seq', 'head'), may hold values from -24 to 24
- block_order: int32 [4], replicated, may hold values from 0 to 3, each once
- valid_frames: int32 [4], replicated, may hold values from 1 to 8, as said below
- noise_steps: int32 [4], replicated, may hold values from 0 to 3
- gate_table: float32 [4, 6144], P(None, 'seq'), may hold values from 1 to 10
- out_weight: bfloat16 [3072, 6144], P('head', 'seq'), may hold values from -0.109375 to 0.109375
- residual: bfloat16 [4, 1280, 6144], P('span', 'head', 'seq'), may hold values from -3 to 3
Outputs:
- mixed: bfloat16 [4, 1280, 6144], P('span', 'head', 'seq')
The draws below stay inside these ranges and needn't reach their ends.
Inputs may be any that keep to these rules, and one draw needn't show every extreme that they name: `valid_frames`: some block has all 8 frames open.
All inputs are finite; a program needn't handle non-finite values.
Results may differ from the reference program's by a relative error of at most 0.017.
Values may be sent and summed in bfloat16 or wider, within the bound.
No kernel may reach another device: no remote copies, remote signals or barrier semaphores. Data moves between devices by JAX's collectives and lax.ppermute only.
A program may use at most 128 MiB of HBM per device.

```python
import math
import jax
import jax.numpy as jnp
from jax import lax

D = 6144
HEADS = 24
HD = 128
FRAMES = 8
STEPS = 4
BLOCKS = 4
BLOCK_TOK = 1280


def draw_query_proj(key, part):
    own_key = jax.random.fold_in(key, 1)
    shape = (BLOCKS, BLOCK_TOK, HEADS * HD)
    return jnp.clip(jax.random.normal(own_key, shape, jnp.float32), -6.0, 6.0).astype(jnp.bfloat16)


def draw_key_proj(key, part):
    own_key = jax.random.fold_in(key, 2)
    shape = (BLOCKS, BLOCK_TOK, HEADS * HD)
    return jnp.clip(jax.random.normal(own_key, shape, jnp.float32), -6.0, 6.0).astype(jnp.bfloat16)


def draw_valid_frames(key, part):
    count_key, pick_key = jax.random.split(jax.random.fold_in(key, 3))
    counts = jax.random.randint(count_key, (BLOCKS,), 1, FRAMES + 1)
    chosen = jax.random.randint(pick_key, (), 0, BLOCKS)
    return jnp.where(jnp.arange(BLOCKS) == chosen, FRAMES, counts).astype(jnp.int32)


def plant(result, rng, least, top_value):
    spot = [jax.random.randint(jax.random.fold_in(rng, axis), (), 0, length) for axis, length in enumerate(result.shape)]
    main_axis = result.shape.index(max(result.shape))
    next_to = spot[:main_axis] + [(spot[main_axis] + 1) % result.shape[main_axis]] + spot[main_axis + 1:]
    return result.at[tuple(spot)].set(least).at[tuple(next_to)].set(top_value)


def shard_levels(stream_key, dims, cuts, smallest, largest):
    factor_of = 1.0
    for position, blocks in cuts:
        steps = jax.random.uniform(jax.random.fold_in(jax.random.fold_in(stream_key, 6), position), (blocks,), jnp.float32, smallest / len(cuts), largest / len(cuts))
        factor_of = factor_of * jnp.repeat(jnp.exp(steps), dims[position] // blocks).reshape((-1,) + (1,) * (len(dims) - 1 - position))
    return factor_of


def scatter_about(key, shape, scale, reach, pieces=(), held_as=jnp.bfloat16):
    level = shard_levels(key, shape, pieces, -0.22, 0.18) if pieces else 1.0
    array = jax.random.normal(key, shape, jnp.float32) * scale * level
    return jnp.minimum(jnp.maximum(array, -reach), reach).astype(held_as)


def setup_inputs(seed: int = 0) -> dict:
    key_list = jax.random.split(jax.random.key(seed), 10)
    query_proj = draw_query_proj(jax.random.fold_in(key_list[9], 71), 0)
    key_proj = draw_key_proj(jax.random.fold_in(key_list[9], 71), 0)
    value_proj = scatter_about(key_list[2], (BLOCKS, BLOCK_TOK, HEADS * HD), 4.0, 24.0, ((0, 4), (1, 32), (2, 4)))
    block_order = jax.random.permutation(key_list[3], BLOCKS).astype(jnp.int32)
    valid_frames = draw_valid_frames(jax.random.fold_in(key_list[9], 71), 0)
    noise_steps = plant(jax.random.randint(key_list[5], (BLOCKS,), 0, STEPS), jax.random.fold_in(key_list[5], 1), 0, STEPS - 1).astype(jnp.int32)
    gate_table = jnp.clip(jnp.exp(math.log(10.0) - 2.3025851 * jax.random.uniform(key_list[6], (STEPS, D), jnp.float32) ** shard_levels(key_list[6], (STEPS, D), ((1, 32),), -0.2, 0.2)), 1.0, 10.0)
    out_weight = scatter_about(key_list[7], (HEADS * HD, D), (HEADS * HD) ** -0.5, 0.109375, ((0, 4), (1, 32)))
    residual = scatter_about(key_list[8], (BLOCKS, BLOCK_TOK, D), 0.5, 3.0, ((0, 4), (1, 4), (2, 32)))
    return {"query_proj": query_proj, "key_proj": key_proj, "value_proj": value_proj, "block_order": block_order, "valid_frames": valid_frames, "noise_steps": noise_steps, "gate_table": gate_table, "out_weight": out_weight, "residual": residual}


floor_score = -1.0e30


def reference(query_proj, key_proj, value_proj, block_order, valid_frames, noise_steps, gate_table, out_weight, residual):
    block_count = query_proj.shape[0]
    block_len = query_proj.shape[1]
    frame_len = block_len // FRAMES
    frame_index = jnp.arange(block_len, dtype=jnp.int32) // frame_len
    frame_open = frame_index[None, :] < valid_frames[:, None]
    queries = query_proj.reshape(block_count, block_len, HEADS, HD)
    keys_all = key_proj.reshape(block_count * block_len, HEADS, HD)
    values_all = value_proj.reshape(block_count * block_len, HEADS, HD)
    score_scale = 1.0 / (HD ** 0.5)

    def one_block(block_number):
        order_here = lax.dynamic_index_in_dim(block_order, block_number, 0, keepdims=False)
        allowed = ((block_order <= order_here)[:, None] & frame_open).reshape(-1)
        query_block = lax.dynamic_index_in_dim(queries, block_number, 0, keepdims=False)

        def one_head(head_number):
            query_head = lax.dynamic_index_in_dim(query_block, head_number, 1, keepdims=False)
            key_head = lax.dynamic_index_in_dim(keys_all, head_number, 1, keepdims=False)
            value_head = lax.dynamic_index_in_dim(values_all, head_number, 1, keepdims=False)
            scores = jnp.dot(query_head, key_head.T, preferred_element_type=jnp.float32) * score_scale
            scores = jnp.where(allowed[None, :], scores, floor_score)
            row_max = jnp.max(scores, axis=1, keepdims=True)
            weights = jnp.where(allowed[None, :], jnp.exp(scores - row_max), 0.0)
            denominator = jnp.sum(weights, axis=1, keepdims=True)
            return jnp.dot(weights.astype(jnp.bfloat16), value_head, preferred_element_type=jnp.float32) / denominator

        heads_out = lax.map(one_head, jnp.arange(HEADS, dtype=jnp.int32))
        return jnp.transpose(heads_out, (1, 0, 2)).reshape(block_len, HEADS * HD).astype(jnp.bfloat16)

    attended = lax.map(one_block, jnp.arange(block_count, dtype=jnp.int32))
    projected = jnp.dot(attended.reshape(block_count * block_len, HEADS * HD), out_weight, preferred_element_type=jnp.float32)
    projected = projected.reshape(block_count, block_len, -1)
    gates = gate_table[noise_steps]
    return (residual.astype(jnp.float32) + gates[:, None, :] * projected).astype(jnp.bfloat16)
```

```python
import jax
import jax.numpy as jnp
from jax import lax
from jax.experimental import pallas as pl
from jax.experimental.pallas import tpu as pltpu
from jax.sharding import Mesh, PartitionSpec as P

HD = 128
FRAMES = 8
CLOSED = -1e30
LOWEST = -1e20
AXES = ("span", "zh", "y", "core", "head")


def attend_kernel(order_ref, valid_ref, q_ref, near_ref, far_ref, out_ref):
    spans = order_ref.shape[0]
    width = q_ref.shape[1]
    heads = width // HD
    rows = q_ref.shape[0]
    slab = near_ref.shape[0] // (2 * spans)
    part = slab // 2
    span = lax.axis_index("span")
    zh = lax.axis_index("zh")
    y = lax.axis_index("y")
    order_here = order_ref[span]
    keys = 2 * spans * slab
    place = lax.broadcasted_iota(jnp.int32, (1, keys), 1)
    place = jnp.where(place >= spans * slab, place - spans * slab, place)
    bias = jnp.zeros((1, keys), jnp.float32)
    frames_half = FRAMES // 2
    for block in range(spans):
        for turn in range(2):
            frame = (zh ^ turn) * frames_half + y // (8 // frames_half)
            is_open = (order_ref[block] <= order_here) & (frame < valid_ref[block])
            least = block * slab + turn * part
            inside = (place >= least) & (place < least + part)
            bias = jnp.where(inside & jnp.logical_not(is_open), CLOSED, bias)
    lane = lax.broadcasted_iota(jnp.int32, (rows, HD), 1)
    stats = jnp.zeros((rows, HD), jnp.float32)
    scale = 1.0 / HD**0.5
    for h in range(heads):
        cols = slice(h * HD, (h + 1) * HD)
        k = jnp.concatenate(
            [ref[2 * b * slab : (2 * b + 1) * slab, cols] for ref in (near_ref, far_ref) for b in range(spans)]
        )
        v = jnp.concatenate(
            [ref[(2 * b + 1) * slab : (2 * b + 2) * slab, cols] for ref in (near_ref, far_ref) for b in range(spans)]
        )
        s = lax.dot_general(q_ref[:, cols], k, (((1,), (1,)), ((), ())), preferred_element_type=jnp.float32)
        s = s * scale + bias
        top = jnp.maximum(jnp.max(s, axis=1, keepdims=True), LOWEST)
        top = top.astype(jnp.bfloat16).astype(jnp.float32)
        w = jnp.exp(s - top)
        total = jnp.sum(w, axis=1, keepdims=True)
        acc = jnp.dot(w.astype(jnp.bfloat16), v, preferred_element_type=jnp.float32)
        out_ref[:, cols] = acc.astype(jnp.bfloat16)
        coarse = total.astype(jnp.bfloat16).astype(jnp.float32)
        stats = jnp.where(lane == h, top, stats)
        stats = jnp.where(lane == heads + h, coarse, stats)
        stats = jnp.where(lane == 2 * heads + h, total - coarse, stats)
    out_ref[:, width:] = stats.astype(jnp.bfloat16)


def combine_kernel(parts_ref, out_ref):
    width = out_ref.shape[2]
    heads = width // HD
    stats = parts_ref[:, :, width:].astype(jnp.float32)
    for h in range(heads):
        cols = slice(h * HD, (h + 1) * HD)
        top = stats[:, :, h : h + 1]
        factor = jnp.exp(top - jnp.max(top, axis=0, keepdims=True))
        total = stats[:, :, heads + h : heads + h + 1] + stats[:, :, 2 * heads + h : 2 * heads + h + 1]
        denominator = jnp.sum(factor * total, axis=0)
        summed = jnp.sum(factor * parts_ref[:, :, cols].astype(jnp.float32), axis=0)
        done = (summed / denominator).astype(jnp.bfloat16)
        for i in range(out_ref.shape[0]):
            out_ref[i, :, cols] = done


def project_kernel(rows_ref, near_ref, far_ref, out_ref):
    zh = lax.axis_index("zh")
    head = lax.axis_index("head")
    half = rows_ref.shape[0] // 2
    for turn, weight in enumerate((near_ref, far_ref)):
        for r in range(2):
            piece = lax.dot_general(
                weight[...],
                rows_ref[r * half : (r + 1) * half, :],
                (((1,), (1,)), ((), ())),
                preferred_element_type=jnp.float32,
            )
            slot = (((zh ^ turn) * 2) + r) ^ head
            out_ref[slot] = piece.astype(jnp.bfloat16)


def shards(q, k, v, block_order, valid_frames, noise_steps, gate_table, out_weight, residual):
    tokens, width = q.shape[1:]
    ny = lax.axis_size("y")
    nx = lax.axis_size("span")
    swap = [(0, 1), (1, 0)]
    vmem = pl.BlockSpec(memory_space=pltpu.VMEM)
    smem = pl.BlockSpec(memory_space=pltpu.SMEM)
    bf16 = jnp.bfloat16
    params = pltpu.CompilerParams(vmem_limit_bytes=48 * 1024 * 1024)

    with jax.named_scope("fetch_kv_zh"):
        kv = jnp.concatenate([k, v])
        kv_far = lax.ppermute(kv, "zh", swap)
    with jax.named_scope("gather_q"):
        queries = lax.all_to_all(jnp.broadcast_to(q, (ny, tokens, width)), "y", 0, 0, tiled=True)
    with jax.named_scope("gather_kv"):
        kv = jnp.stack([kv[0], kv_far[0], kv[1], kv_far[1]])
        near = lax.all_gather(kv, "span", axis=0, tiled=True).reshape(nx * 4 * tokens, width)
        far = lax.ppermute(near, "core", swap)
    with jax.named_scope("fetch_weight"):
        weight = out_weight.T
        weight_far = lax.ppermute(weight, "zh", swap)
    parts = pl.pallas_call(
        attend_kernel,
        out_shape=jax.ShapeDtypeStruct((ny * tokens, width + HD), bf16),
        in_specs=[smem, smem, vmem, vmem, vmem],
        out_specs=vmem,
        compiler_params=params,
        name="attend",
    )(block_order, valid_frames, queries.reshape(ny * tokens, width), near, far)
    with jax.named_scope("return_parts"):
        parts = lax.all_to_all(parts.reshape(ny, tokens, width + HD), "y", 0, 0, tiled=True)
    attended = pl.pallas_call(
        combine_kernel,
        out_shape=jax.ShapeDtypeStruct((ny, tokens, width), bf16),
        in_specs=[vmem],
        out_specs=vmem,
        compiler_params=params,
        name="combine",
    )(parts)
    with jax.named_scope("gather_attended"):
        attended = lax.all_to_all(attended, "y", 0, 0, tiled=True)
        attended = lax.all_gather(attended, "core", axis=1, tiled=True).reshape(2 * ny * tokens, width)
    cols = weight.shape[0]
    pieces = pl.pallas_call(
        project_kernel,
        out_shape=jax.ShapeDtypeStruct((4, cols, ny * tokens), bf16),
        in_specs=[vmem, vmem, vmem],
        out_specs=vmem,
        compiler_params=params,
        name="project",
    )(attended, weight, weight_far)
    with jax.named_scope("sum_heads"):
        total = None
        for i in range(4):
            hops = []
            for zh in range(2):
                for head in range(4):
                    j = i ^ head
                    hops.append((zh * 4 + head, (j >> 1) * 4 + 2 * zh + (j & 1)))
            got = lax.ppermute(pieces[i], ("zh", "head"), hops).astype(jnp.float32)
            total = got if total is None else total + got
    with jax.named_scope("finish"):
        block = lax.axis_index("span")
        step = jnp.sum(jnp.where(jnp.arange(noise_steps.shape[0]) == block, noise_steps, 0))
        chosen = jnp.arange(gate_table.shape[0]) == step
        gate = jnp.sum(jnp.where(chosen[:, None], gate_table, 0.0), axis=0)
        mixed = (residual[0].T.astype(jnp.float32) + gate[:, None] * total).astype(bf16)
    return mixed.T[None]


def solution(mesh):
    fine = Mesh(mesh.devices.reshape(4, 2, 8, 2, 4), AXES)
    seq = ("zh", "y", "core")
    placed = (
        P("span", seq, "head"),
        P("span", seq, "head"),
        P("span", seq, "head"),
        P(),
        P(),
        P(),
        P(None, seq),
        P("head", seq),
        P("span", "head", seq),
    )
    return jax.shard_map(
        shards, mesh=fine, in_specs=placed, out_specs=P("span", "head", seq), check_vma=False
    )
```

```python
import jax
import jax.numpy as jnp
from jax import lax
from jax.experimental import pallas as pl
from jax.experimental.pallas import tpu as pltpu
from jax.sharding import Mesh, PartitionSpec as P

HD = 128
CLOSED = -1e30
LOWEST = -1e20
AXES = ("span", "zh", "y2", "y1", "y0", "core", "head")
FRAME = ("zh", "y2", "y1")


def attend_kernel(order_ref, valid_ref, q_ref, near_ref, far_ref, out_ref):
    blocks = order_ref.shape[0]
    rows, width = q_ref.shape
    heads = width // HD
    slab = near_ref.shape[0] // (2 * blocks)
    frame = lax.axis_index("zh") * 4 + lax.axis_index("y2") * 2 + lax.axis_index("y1")
    order_here = order_ref[lax.axis_index("span")]
    place = lax.broadcasted_iota(jnp.int32, (1, 2 * blocks * slab), 1)
    place = jnp.where(place >= blocks * slab, place - blocks * slab, place)
    bias = jnp.zeros(place.shape, jnp.float32)
    for block in range(blocks):
        is_open = (order_ref[block] <= order_here) & (frame < valid_ref[block])
        inside = (place >= block * slab) & (place < (block + 1) * slab)
        bias = jnp.where(inside & jnp.logical_not(is_open), CLOSED, bias)
    lane = lax.broadcasted_iota(jnp.int32, (rows, HD), 1)
    stats = jnp.zeros((rows, HD), jnp.float32)
    scale = 1.0 / HD**0.5
    for h in range(heads):
        cols = slice(h * HD, (h + 1) * HD)
        k = jnp.concatenate(
            [ref[2 * b * slab : (2 * b + 1) * slab, cols] for ref in (near_ref, far_ref) for b in range(blocks)]
        )
        v = jnp.concatenate(
            [ref[(2 * b + 1) * slab : (2 * b + 2) * slab, cols] for ref in (near_ref, far_ref) for b in range(blocks)]
        )
        s = lax.dot_general(q_ref[:, cols], k, (((1,), (1,)), ((), ())), preferred_element_type=jnp.float32)
        s = s * scale + bias
        top = jnp.maximum(jnp.max(s, axis=1, keepdims=True), LOWEST)
        top = top.astype(jnp.bfloat16).astype(jnp.float32)
        w = jnp.exp(s - top)
        total = jnp.sum(w, axis=1, keepdims=True)
        acc = jnp.dot(w.astype(jnp.bfloat16), v, preferred_element_type=jnp.float32)
        out_ref[:, cols] = acc.astype(jnp.bfloat16)
        coarse = total.astype(jnp.bfloat16).astype(jnp.float32)
        stats = jnp.where(lane == h, top, stats)
        stats = jnp.where(lane == heads + h, coarse, stats)
        stats = jnp.where(lane == 2 * heads + h, total - coarse, stats)
    out_ref[:, width:] = stats.astype(jnp.bfloat16)


def combine_kernel(parts_ref, out_ref):
    width = out_ref.shape[2]
    heads = width // HD
    stats = parts_ref[:, :, width:].astype(jnp.float32)
    for h in range(heads):
        cols = slice(h * HD, (h + 1) * HD)
        top = stats[:, :, h : h + 1]
        factor = jnp.exp(top - jnp.max(top, axis=0, keepdims=True))
        total = stats[:, :, heads + h : heads + h + 1] + stats[:, :, 2 * heads + h : 2 * heads + h + 1]
        denominator = jnp.sum(factor * total, axis=0)
        summed = jnp.sum(factor * parts_ref[:, :, cols].astype(jnp.float32), axis=0)
        done = (summed / denominator).astype(jnp.bfloat16)
        for i in range(out_ref.shape[0]):
            out_ref[i, :, cols] = done


def project_kernel(rows_ref, near_ref, far_ref, out_ref):
    y0 = lax.axis_index("y0")
    chunks = out_ref.shape[0] // 2
    rows = rows_ref.shape[0] // chunks
    half = rows // 2
    for turn, weight in enumerate((near_ref, far_ref)):
        for chunk in range(chunks):
            piece = lax.dot_general(
                rows_ref[chunk * rows : (chunk + 1) * rows, :],
                weight[...],
                (((1,), (1,)), ((), ())),
                preferred_element_type=jnp.float32,
            )
            slot = chunk * 2 + (y0 ^ turn)
            out_ref[slot, :rows, :] = piece[:, :HD].astype(jnp.bfloat16)
            tail = jnp.concatenate([piece[:half, HD:], piece[half:, HD:]], axis=1)
            out_ref[slot, rows:, :] = tail.astype(jnp.bfloat16)


def finish_kernel(steps_ref, pieces_ref, gate_ref, residual_ref, out_ref):
    step = steps_ref[lax.axis_index("span")]
    gate = gate_ref[pl.ds(step, 1), :]
    rows = residual_ref.shape[1] // 2
    half = rows // 2
    sums = []
    for y0 in range(2):
        total = pieces_ref[y0].astype(jnp.float32)
        for head in range(1, 4):
            total = total + pieces_ref[2 * head + y0].astype(jnp.float32)
        sums.append(total)
    near, far = sums
    main = jnp.concatenate([near[:half], far[:half], near[half:rows], far[half:rows]])
    rest = HD // 2
    tail = jnp.concatenate([near[rows:, :rest], far[rows:, :rest], near[rows:, rest:], far[rows:, rest:]])
    main = (main * gate[:, :HD]).T
    tail = (tail * gate[:, HD:]).T
    out_ref[:HD, :] = (residual_ref[:HD, :].astype(jnp.float32) + main).astype(jnp.bfloat16)
    out_ref[HD:, :] = (residual_ref[HD:, :].astype(jnp.float32) + tail).astype(jnp.bfloat16)


def shards(q, k, v, block_order, valid_frames, noise_steps, gate_table, out_weight, residual):
    tokens, width = q.shape[1:]
    parts_n = 8
    nx = lax.axis_size("span")
    swap = [(0, 1), (1, 0)]
    vmem = pl.BlockSpec(memory_space=pltpu.VMEM)
    smem = pl.BlockSpec(memory_space=pltpu.SMEM)
    bf16 = jnp.bfloat16
    params = pltpu.CompilerParams(vmem_limit_bytes=48 * 1024 * 1024)

    with jax.named_scope("fetch_kv"):
        kv = jnp.concatenate([k, v])
        kv_far = lax.ppermute(kv, "y0", swap)
    with jax.named_scope("gather_q"):
        queries = lax.all_to_all(jnp.broadcast_to(q, (parts_n, tokens, width)), FRAME, 0, 0, tiled=True)
    with jax.named_scope("gather_kv"):
        kv = jnp.stack([kv[0], kv_far[0], kv[1], kv_far[1]])
        near = lax.all_gather(kv, "span", axis=0, tiled=True).reshape(nx * 4 * tokens, width)
        far = lax.ppermute(near, "core", swap)
    with jax.named_scope("fetch_weight"):
        weight = out_weight.T
        weight_far = lax.ppermute(weight, "y0", swap)
    parts = pl.pallas_call(
        attend_kernel,
        out_shape=jax.ShapeDtypeStruct((parts_n * tokens, width + HD), bf16),
        in_specs=[smem, smem, vmem, vmem, vmem],
        out_specs=vmem,
        compiler_params=params,
        name="attend",
    )(block_order, valid_frames, queries.reshape(parts_n * tokens, width), near, far)
    with jax.named_scope("return_parts"):
        parts = lax.all_to_all(parts.reshape(parts_n, tokens, width + HD), FRAME, 0, 0, tiled=True)
    attended = pl.pallas_call(
        combine_kernel,
        out_shape=jax.ShapeDtypeStruct((parts_n, tokens, width), bf16),
        in_specs=[vmem],
        out_specs=vmem,
        compiler_params=params,
        name="combine",
    )(parts)
    with jax.named_scope("gather_attended"):
        attended = lax.all_to_all(attended, FRAME, 0, 0, tiled=True)
        attended = lax.all_gather(attended, "core", axis=1, tiled=True).reshape(2 * parts_n * tokens, width)
    cols = weight.shape[0]
    slot_rows = 4 * tokens * cols // HD
    pieces = pl.pallas_call(
        project_kernel,
        out_shape=jax.ShapeDtypeStruct((8, slot_rows, HD), bf16),
        in_specs=[vmem, vmem, vmem],
        out_specs=vmem,
        compiler_params=params,
        name="project",
    )(attended, weight, weight_far)
    with jax.named_scope("sum_heads"):
        pieces = lax.all_to_all(pieces, ("head", "y0"), 0, 0, tiled=True)
    mixed = pl.pallas_call(
        finish_kernel,
        out_shape=jax.ShapeDtypeStruct(residual.shape[:0:-1], bf16),
        in_specs=[smem, vmem, vmem, vmem],
        out_specs=vmem,
        compiler_params=params,
        name="finish",
    )(noise_steps, pieces, gate_table, residual[0].T)
    return mixed.T[None]


def solution(mesh):
    fine = Mesh(mesh.devices.reshape(4, 2, 2, 2, 2, 2, 4), AXES)
    seq = ("zh", "y2", "y1", "y0", "core")
    placed = (
        P("span", seq, "head"),
        P("span", seq, "head"),
        P("span", seq, "head"),
        P(),
        P(),
        P(),
        P(None, seq),
        P("head", seq),
        P("span", "head", seq),
    )
    return jax.shard_map(
        shards, mesh=fine, in_specs=placed, out_specs=P("span", "head", seq), check_vma=False
    )
```

```python
import jax
import jax.numpy as jnp
from jax import lax
from jax.experimental import pallas as pl
from jax.experimental.pallas import tpu as pltpu
from jax.sharding import Mesh, PartitionSpec as P

HD = 128
CLOSED = -1e30
LOWEST = -1e20
AXES = ("span", "zh", "y", "core", "head")
FRAMES = 8


def attend_kernel(order_ref, valid_ref, q_ref, keys_ref, values_ref, out_ref):
    blocks = order_ref.shape[0]
    rows, width = q_ref.shape
    heads = width // HD
    count = keys_ref.shape[0]
    slab = count // (2 * blocks)
    zh = lax.axis_index("zh")
    y = lax.axis_index("y")
    order_here = order_ref[lax.axis_index("span")]
    place = lax.broadcasted_iota(jnp.int32, (1, count), 1)
    place = jnp.where(place >= blocks * slab, place - blocks * slab, place)
    bias = jnp.zeros(place.shape, jnp.float32)
    for block in range(blocks):
        for turn in range(2):
            frame = (zh ^ turn) * (FRAMES // 2) + y // 2
            is_open = (order_ref[block] <= order_here) & (frame < valid_ref[block])
            least = block * slab + turn * (slab // 2)
            inside = (place >= least) & (place < least + slab // 2)
            bias = jnp.where(inside & jnp.logical_not(is_open), CLOSED, bias)
    lane = lax.broadcasted_iota(jnp.int32, (rows, HD), 1)
    stats = jnp.zeros((rows, HD), jnp.float32)
    scale = 1.0 / HD**0.5
    for h in range(heads):
        cols = slice(h * HD, (h + 1) * HD)
        s = lax.dot_general(
            q_ref[:, cols], keys_ref[:, cols], (((1,), (1,)), ((), ())), preferred_element_type=jnp.float32
        )
        s = s * scale + bias
        top = jnp.maximum(jnp.max(s, axis=1, keepdims=True), LOWEST)
        top = top.astype(jnp.bfloat16).astype(jnp.float32)
        w = jnp.exp(s - top)
        total = jnp.sum(w, axis=1, keepdims=True)
        acc = jnp.dot(w.astype(jnp.bfloat16), values_ref[:, cols], preferred_element_type=jnp.float32)
        out_ref[:, cols] = acc.astype(jnp.bfloat16)
        coarse = total.astype(jnp.bfloat16).astype(jnp.float32)
        stats = jnp.where(lane == h, top, stats)
        stats = jnp.where(lane == heads + h, coarse, stats)
        stats = jnp.where(lane == 2 * heads + h, total - coarse, stats)
    out_ref[:, width:] = stats.astype(jnp.bfloat16)


def combine_kernel(parts_ref, out_ref):
    width = out_ref.shape[2]
    heads = width // HD
    stats = parts_ref[:, :, width:].astype(jnp.float32)
    for h in range(heads):
        cols = slice(h * HD, (h + 1) * HD)
        top = stats[:, :, h : h + 1]
        factor = jnp.exp(top - jnp.max(top, axis=0, keepdims=True))
        total = stats[:, :, heads + h : heads + h + 1] + stats[:, :, 2 * heads + h : 2 * heads + h + 1]
        denominator = jnp.sum(factor * total, axis=0)
        summed = jnp.sum(factor * parts_ref[:, :, cols].astype(jnp.float32), axis=0)
        done = (summed / denominator).astype(jnp.bfloat16)
        for i in range(out_ref.shape[0]):
            out_ref[i, :, cols] = done


def project_kernel(rows_ref, near_ref, far_ref, out_ref):
    zh = lax.axis_index("zh")
    rows = rows_ref.shape[0] // 2
    half = rows // 2
    for turn, weight in enumerate((near_ref, far_ref)):
        for r in range(2):
            piece = lax.dot_general(
                rows_ref[r * rows : (r + 1) * rows, :],
                weight[...],
                (((1,), (1,)), ((), ())),
                preferred_element_type=jnp.float32,
            )
            slot = 4 * (zh ^ turn) + 2 * zh + r
            out_ref[slot, :rows, :] = piece[:, :HD].astype(jnp.bfloat16)
            tail = jnp.concatenate([piece[:half, HD:], piece[half:, HD:]], axis=1)
            out_ref[slot, rows:, :] = tail.astype(jnp.bfloat16)


def finish_kernel(steps_ref, pieces_ref, gate_ref, residual_ref, out_ref):
    step = steps_ref[lax.axis_index("span")]
    gate = gate_ref[pl.ds(step, 1), :]
    rows = residual_ref.shape[1]
    first = 4 * (lax.axis_index("head") // 2)
    total = pieces_ref[first].astype(jnp.float32)
    for head in range(1, 4):
        total = total + pieces_ref[first + head].astype(jnp.float32)
    main = total[:rows]
    tail = jnp.concatenate([total[rows:, : HD // 2], total[rows:, HD // 2 :]])
    main = (main * gate[:, :HD]).T
    tail = (tail * gate[:, HD:]).T
    out_ref[:HD, :] = (residual_ref[:HD, :].astype(jnp.float32) + main).astype(jnp.bfloat16)
    out_ref[HD:, :] = (residual_ref[HD:, :].astype(jnp.float32) + tail).astype(jnp.bfloat16)


def shards(q, k, v, block_order, valid_frames, noise_steps, gate_table, out_weight, residual):
    tokens, width = q.shape[1:]
    parts_n = lax.axis_size("y")
    nx = lax.axis_size("span")
    swap = [(0, 1), (1, 0)]
    vmem = pl.BlockSpec(memory_space=pltpu.VMEM)
    smem = pl.BlockSpec(memory_space=pltpu.SMEM)
    bf16 = jnp.bfloat16
    params = pltpu.CompilerParams(vmem_limit_bytes=48 * 1024 * 1024)

    with jax.named_scope("fetch_kv"):
        kv = jnp.concatenate([k, v])
        kv_far = lax.ppermute(kv, "zh", swap)
    with jax.named_scope("gather_q"):
        queries = lax.all_to_all(jnp.broadcast_to(q, (parts_n, tokens, width)), "y", 0, 0, tiled=True)
    with jax.named_scope("gather_kv"):
        kv = jnp.stack([kv[0], kv_far[0], kv[1], kv_far[1]])
        kv = kv.reshape(2, 2 * tokens, width)
        near = lax.all_gather(kv, "span", axis=1, tiled=True)
        keys = lax.all_gather(near[0], "core", axis=0, tiled=True)
        values = lax.all_gather(near[1], "core", axis=0, tiled=True)
    with jax.named_scope("fetch_weight"):
        weight = out_weight.T
        weight_far = lax.ppermute(weight, "zh", swap)
    parts = pl.pallas_call(
        attend_kernel,
        out_shape=jax.ShapeDtypeStruct((parts_n * tokens, width + HD), bf16),
        in_specs=[smem, smem, vmem, vmem, vmem],
        out_specs=vmem,
        compiler_params=params,
        name="attend",
    )(block_order, valid_frames, queries.reshape(parts_n * tokens, width), keys, values)
    with jax.named_scope("return_parts"):
        parts = lax.all_to_all(parts.reshape(parts_n, tokens, width + HD), "y", 0, 0, tiled=True)
    attended = pl.pallas_call(
        combine_kernel,
        out_shape=jax.ShapeDtypeStruct((parts_n, tokens, width), bf16),
        in_specs=[vmem],
        out_specs=vmem,
        compiler_params=params,
        name="combine",
    )(parts)
    with jax.named_scope("gather_attended"):
        attended = lax.all_to_all(attended, "y", 0, 0, tiled=True)
        attended = lax.all_gather(attended, "core", axis=1, tiled=True).reshape(2 * parts_n * tokens, width)
    cols = weight.shape[0]
    slot_rows = parts_n * tokens * cols // HD
    pieces = pl.pallas_call(
        project_kernel,
        out_shape=jax.ShapeDtypeStruct((8, slot_rows, HD), bf16),
        in_specs=[vmem, vmem, vmem],
        out_specs=vmem,
        compiler_params=params,
        name="project",
    )(attended, weight, weight_far)
    with jax.named_scope("sum_heads"):
        pieces = lax.all_to_all(pieces, ("zh", "head"), 0, 0, tiled=True)
    mixed = pl.pallas_call(
        finish_kernel,
        out_shape=jax.ShapeDtypeStruct(residual.shape[:0:-1], bf16),
        in_specs=[smem, vmem, vmem, vmem],
        out_specs=vmem,
        compiler_params=params,
        name="finish",
    )(noise_steps, pieces, gate_table, residual[0].T)
    return mixed.T[None]


def solution(mesh):
    fine = Mesh(mesh.devices.reshape(4, 2, 8, 2, 4), AXES)
    seq = ("zh", "y", "core")
    placed = (
        P("span", seq, "head"),
        P("span", seq, "head"),
        P("span", seq, "head"),
        P(),
        P(),
        P(),
        P(None, seq),
        P("head", seq),
        P("span", "head", seq),
    )
    return jax.shard_map(
        shards, mesh=fine, in_specs=placed, out_specs=P("span", "head", seq), check_vma=False
    )
```

```python
import jax
import jax.numpy as jnp
from jax import lax
from jax.experimental import pallas as pl
from jax.experimental.pallas import tpu as pltpu
from jax.sharding import Mesh, PartitionSpec as P

HD = 128
CLOSED = -1e30
LOWEST = -1e20
AXES = ("span", "zh", "y2", "y1", "y0", "core", "head")
ROW = ("y2", "y1", "y0")
FRAME = ("zh", "y2", "y1")
FRAMES = 8


def attend_kernel(order_ref, valid_ref, q_ref, keys_ref, values_ref, out_ref):
    blocks = order_ref.shape[0]
    rows, width = q_ref.shape
    heads = width // HD
    count = keys_ref.shape[0]
    slab = count // (2 * blocks)
    zh = lax.axis_index("zh")
    y = lax.axis_index("y2") * 4 + lax.axis_index("y1") * 2 + lax.axis_index("y0")
    order_here = order_ref[lax.axis_index("span")]
    place = lax.broadcasted_iota(jnp.int32, (1, count), 1)
    place = jnp.where(place >= blocks * slab, place - blocks * slab, place)
    bias = jnp.zeros(place.shape, jnp.float32)
    for block in range(blocks):
        for turn in range(2):
            frame = (zh ^ turn) * (FRAMES // 2) + y // 2
            is_open = (order_ref[block] <= order_here) & (frame < valid_ref[block])
            least = block * slab + turn * (slab // 2)
            inside = (place >= least) & (place < least + slab // 2)
            bias = jnp.where(inside & jnp.logical_not(is_open), CLOSED, bias)
    lane = lax.broadcasted_iota(jnp.int32, (rows, HD), 1)
    stats = jnp.zeros((rows, HD), jnp.float32)
    scale = 1.0 / HD**0.5
    for h in range(heads):
        cols = slice(h * HD, (h + 1) * HD)
        s = lax.dot_general(
            q_ref[:, cols], keys_ref[:, cols], (((1,), (1,)), ((), ())), preferred_element_type=jnp.float32
        )
        s = s * scale + bias
        top = jnp.maximum(jnp.max(s, axis=1, keepdims=True), LOWEST)
        top = top.astype(jnp.bfloat16).astype(jnp.float32)
        w = jnp.exp(s - top)
        total = jnp.sum(w, axis=1, keepdims=True)
        acc = jnp.dot(w.astype(jnp.bfloat16), values_ref[:, cols], preferred_element_type=jnp.float32)
        out_ref[:, cols] = acc.astype(jnp.bfloat16)
        coarse = total.astype(jnp.bfloat16).astype(jnp.float32)
        stats = jnp.where(lane == h, top, stats)
        stats = jnp.where(lane == heads + h, coarse, stats)
        stats = jnp.where(lane == 2 * heads + h, total - coarse, stats)
    out_ref[:, width:] = stats.astype(jnp.bfloat16)


def combine_kernel(parts_ref, out_ref):
    width = out_ref.shape[2]
    heads = width // HD
    stats = parts_ref[:, :, width:].astype(jnp.float32)
    for h in range(heads):
        cols = slice(h * HD, (h + 1) * HD)
        top = stats[:, :, h : h + 1]
        factor = jnp.exp(top - jnp.max(top, axis=0, keepdims=True))
        total = stats[:, :, heads + h : heads + h + 1] + stats[:, :, 2 * heads + h : 2 * heads + h + 1]
        denominator = jnp.sum(factor * total, axis=0)
        summed = jnp.sum(factor * parts_ref[:, :, cols].astype(jnp.float32), axis=0)
        done = (summed / denominator).astype(jnp.bfloat16)
        for i in range(out_ref.shape[0]):
            out_ref[i, :, cols] = done


def project_kernel(rows_ref, near_ref, far_ref, out_ref):
    y0 = lax.axis_index("y0")
    chunks = out_ref.shape[0] // 2
    rows = rows_ref.shape[0] // chunks
    half = rows // 2
    for turn, weight in enumerate((near_ref, far_ref)):
        for chunk in range(chunks):
            piece = lax.dot_general(
                rows_ref[chunk * rows : (chunk + 1) * rows, :],
                weight[...],
                (((1,), (1,)), ((), ())),
                preferred_element_type=jnp.float32,
            )
            slot = chunk * 2 + (y0 ^ turn)
            out_ref[slot, :rows, :] = piece[:, :HD].astype(jnp.bfloat16)
            tail = jnp.concatenate([piece[:half, HD:], piece[half:, HD:]], axis=1)
            out_ref[slot, rows:, :] = tail.astype(jnp.bfloat16)


def finish_kernel(steps_ref, pieces_ref, gate_ref, residual_ref, out_ref):
    step = steps_ref[lax.axis_index("span")]
    gate = gate_ref[pl.ds(step, 1), :]
    rows = residual_ref.shape[1] // 2
    half = rows // 2
    sums = []
    for y0 in range(2):
        total = pieces_ref[y0].astype(jnp.float32)
        for head in range(1, 4):
            total = total + pieces_ref[2 * head + y0].astype(jnp.float32)
        sums.append(total)
    near, far = sums
    main = jnp.concatenate([near[:half], far[:half], near[half:rows], far[half:rows]])
    rest = HD // 2
    tail = jnp.concatenate([near[rows:, :rest], far[rows:, :rest], near[rows:, rest:], far[rows:, rest:]])
    main = (main * gate[:, :HD]).T
    tail = (tail * gate[:, HD:]).T
    out_ref[:HD, :] = (residual_ref[:HD, :].astype(jnp.float32) + main).astype(jnp.bfloat16)
    out_ref[HD:, :] = (residual_ref[HD:, :].astype(jnp.float32) + tail).astype(jnp.bfloat16)


def shards(q, k, v, block_order, valid_frames, noise_steps, gate_table, out_weight, residual):
    tokens, width = q.shape[1:]
    parts_n = lax.axis_size(ROW)
    nx = lax.axis_size("span")
    swap = [(0, 1), (1, 0)]
    vmem = pl.BlockSpec(memory_space=pltpu.VMEM)
    smem = pl.BlockSpec(memory_space=pltpu.SMEM)
    bf16 = jnp.bfloat16
    params = pltpu.CompilerParams(vmem_limit_bytes=48 * 1024 * 1024)

    with jax.named_scope("fetch_kv"):
        kv = jnp.concatenate([k, v])
        kv_far = lax.ppermute(kv, "zh", swap)
    with jax.named_scope("gather_q"):
        queries = lax.all_to_all(jnp.broadcast_to(q, (parts_n, tokens, width)), ROW, 0, 0, tiled=True)
    with jax.named_scope("gather_kv"):
        kv = jnp.stack([kv[0], kv_far[0], kv[1], kv_far[1]])
        kv = kv.reshape(2, 2 * tokens, width)
        near = lax.all_gather(kv, "span", axis=1, tiled=True)
        keys = lax.all_gather(near[0], "core", axis=0, tiled=True)
        values = lax.all_gather(near[1], "core", axis=0, tiled=True)
    with jax.named_scope("fetch_weight"):
        weight = out_weight.T
        weight_far = lax.ppermute(weight, "y0", swap)
    parts = pl.pallas_call(
        attend_kernel,
        out_shape=jax.ShapeDtypeStruct((parts_n * tokens, width + HD), bf16),
        in_specs=[smem, smem, vmem, vmem, vmem],
        out_specs=vmem,
        compiler_params=params,
        name="attend",
    )(block_order, valid_frames, queries.reshape(parts_n * tokens, width), keys, values)
    with jax.named_scope("return_parts"):
        parts = lax.all_to_all(parts.reshape(parts_n, tokens, width + HD), ROW, 0, 0, tiled=True)
    attended = pl.pallas_call(
        combine_kernel,
        out_shape=jax.ShapeDtypeStruct((parts_n, tokens, width), bf16),
        in_specs=[vmem],
        out_specs=vmem,
        compiler_params=params,
        name="combine",
    )(parts)
    with jax.named_scope("gather_attended"):
        attended = lax.all_to_all(attended, FRAME, 0, 0, tiled=True)
        attended = lax.all_gather(attended, "core", axis=1, tiled=True).reshape(2 * parts_n * tokens, width)
    cols = weight.shape[0]
    slot_rows = 4 * tokens * cols // HD
    pieces = pl.pallas_call(
        project_kernel,
        out_shape=jax.ShapeDtypeStruct((8, slot_rows, HD), bf16),
        in_specs=[vmem, vmem, vmem],
        out_specs=vmem,
        compiler_params=params,
        name="project",
    )(attended, weight, weight_far)
    with jax.named_scope("sum_heads"):
        pieces = lax.all_to_all(pieces, ("head", "y0"), 0, 0, tiled=True)
    mixed = pl.pallas_call(
        finish_kernel,
        out_shape=jax.ShapeDtypeStruct(residual.shape[:0:-1], bf16),
        in_specs=[smem, vmem, vmem, vmem],
        out_specs=vmem,
        compiler_params=params,
        name="finish",
    )(noise_steps, pieces, gate_table, residual[0].T)
    return mixed.T[None]


def solution(mesh):
    fine = Mesh(mesh.devices.reshape(4, 2, 2, 2, 2, 2, 4), AXES)
    seq = ("zh",) + ROW + ("core",)
    placed = (
        P("span", seq, "head"),
        P("span", seq, "head"),
        P("span", seq, "head"),
        P(),
        P(),
        P(),
        P(None, seq),
        P("head", seq),
        P("span", "head", seq),
    )
    return jax.shard_map(
        shards, mesh=fine, in_specs=placed, out_specs=P("span", "head", seq), check_vma=False
    )
```

```python
import jax
import jax.numpy as jnp
from jax import lax
from jax.experimental import pallas as pl
from jax.experimental.pallas import tpu as pltpu
from jax.sharding import Mesh, PartitionSpec as P

HD = 128
CLOSED = -1e30
LOWEST = -1e20
AXES = ("span", "zh", "y2", "y1", "y0", "core", "head")
ROW = ("y2", "y1", "y0")
FRAME = ("zh", "y2", "y1")
FRAMES = 8


def pack_kernel(q_ref, k_ref, v_ref, out_ref):
    heads = q_ref.shape[1] // HD
    for h in range(out_ref.shape[0]):
        for i, ref in enumerate((q_ref, k_ref, v_ref)):
            if h < heads:
                out_ref[h, i] = ref[:, h * HD : (h + 1) * HD]
            else:
                out_ref[h, i] = jnp.zeros(out_ref.shape[2:], out_ref.dtype)


def attend_kernel(order_ref, valid_ref, q_ref, near_ref, far_ref, out_ref):
    blocks, rows = q_ref.shape[:2]
    zh = lax.axis_index("zh")
    span = lax.axis_index("span")
    keys = jnp.concatenate([ref[i] for ref in (near_ref, far_ref) for i in (0, 2)])
    values = jnp.concatenate([ref[i] for ref in (near_ref, far_ref) for i in (1, 3)])
    place = lax.broadcasted_iota(jnp.int32, (1, 4 * rows), 1)
    inner = place
    for i in range(1, 4):
        inner = jnp.where(place >= i * rows, place - i * rows, inner)
    half = FRAMES // 2
    frame_rows = rows // half
    near_limit = (valid_ref[span] - half * zh) * frame_rows
    far_limit = (valid_ref[span] - half * (1 - zh)) * frame_rows
    limit = jnp.where(place < 2 * rows, near_limit, far_limit)
    bias = jnp.where(inner < limit, 0.0, CLOSED)
    lane = lax.broadcasted_iota(jnp.int32, (rows, HD), 1)
    scale = 1.0 / HD**0.5
    for block in range(blocks):
        is_open = order_ref[span] <= order_ref[block]

        @pl.when(is_open)
        def _():
            s = lax.dot_general(q_ref[block], keys, (((1,), (1,)), ((), ())), preferred_element_type=jnp.float32)
            s = s * scale + bias
            top = jnp.maximum(jnp.max(s, axis=1, keepdims=True), LOWEST)
            top = top.astype(jnp.bfloat16).astype(jnp.float32)
            w = jnp.exp(s - top)
            total = jnp.sum(w, axis=1, keepdims=True)
            acc = jnp.dot(w.astype(jnp.bfloat16), values, preferred_element_type=jnp.float32)
            coarse = total.astype(jnp.bfloat16).astype(jnp.float32)
            stats = jnp.where(lane == 0, top, jnp.where(lane == 1, coarse, total - coarse))
            out_ref[block, :, :HD] = acc.astype(jnp.bfloat16)
            out_ref[block, :, HD:] = stats.astype(jnp.bfloat16)

        @pl.when(jnp.logical_not(is_open))
        def _():
            out_ref[block, :, :HD] = jnp.zeros((rows, HD), jnp.bfloat16)
            out_ref[block, :, HD:] = jnp.where(lane == 0, LOWEST, 0.0).astype(jnp.bfloat16)


def combine_kernel(parts_ref, near_ref, send_ref):
    stats = parts_ref[:, :, HD:].astype(jnp.float32)
    top = stats[:, :, 0:1]
    factor = jnp.exp(top - jnp.max(top, axis=0, keepdims=True))
    denominator = jnp.sum(factor * (stats[:, :, 1:2] + stats[:, :, 2:3]), axis=0)
    summed = jnp.sum(factor * parts_ref[:, :, :HD].astype(jnp.float32), axis=0)
    done = summed / denominator
    tokens = done.shape[0] // FRAMES
    for y0 in range(2):
        piece = jnp.concatenate([done[(2 * i + y0) * tokens : (2 * i + y0 + 1) * tokens] for i in range(FRAMES // 2)])
        piece = piece.astype(jnp.bfloat16)
        send_ref[y0] = piece
        for i in range(FRAMES // 2):
            near_ref[2 * i + y0] = piece


def project_kernel(near_rows_ref, far_rows_ref, near_ref, far_ref, out_ref):
    zh = lax.axis_index("zh")
    y0 = lax.axis_index("y0")
    heads = near_ref.shape[1] // HD
    slots = near_rows_ref.shape[0] // 2
    rows = near_rows_ref.shape[1]
    quarter = rows // 4
    for side, rows_ref in enumerate((near_rows_ref, far_rows_ref)):
        left = [jnp.concatenate([rows_ref[c * slots + h] for h in range(heads)], axis=1) for c in range(2)]
        for turn, weight in enumerate((near_ref, far_ref)):
            first, second = [
                lax.dot_general(part, weight[...], (((1,), (1,)), ((), ())), preferred_element_type=jnp.float32)
                for part in left
            ]
            for y2 in range(2):
                a, b = 2 * y2 * quarter, (2 * y2 + 1) * quarter
                piece = jnp.concatenate(
                    [first[a : a + quarter], second[a : a + quarter], first[b : b + quarter], second[b : b + quarter]]
                )
                slot = (2 * (zh ^ side) + y2) * 2 + (y0 ^ turn)
                out_ref[slot, :rows, :] = piece[:, :HD].astype(jnp.bfloat16)
                tail = jnp.concatenate([piece[: rows // 2, HD:], piece[rows // 2 :, HD:]], axis=1)
                out_ref[slot, rows:, :] = tail.astype(jnp.bfloat16)


def finish_kernel(steps_ref, pieces_ref, gate_ref, residual_ref, out_ref):
    step = steps_ref[lax.axis_index("span")]
    gate = gate_ref[pl.ds(step, 1), :]
    rows = residual_ref.shape[1] // 2
    half = rows // 2
    sums = []
    for y0 in range(2):
        total = pieces_ref[y0].astype(jnp.float32)
        for head in range(1, 4):
            total = total + pieces_ref[2 * head + y0].astype(jnp.float32)
        sums.append(total)
    near, far = sums
    main = jnp.concatenate([near[:half], far[:half], near[half:rows], far[half:rows]])
    rest = HD // 2
    tail = jnp.concatenate([near[rows:, :rest], far[rows:, :rest], near[rows:, rest:], far[rows:, rest:]])
    main = (main * gate[:, :HD]).T
    tail = (tail * gate[:, HD:]).T
    out_ref[:HD, :] = (residual_ref[:HD, :].astype(jnp.float32) + main).astype(jnp.bfloat16)
    out_ref[HD:, :] = (residual_ref[HD:, :].astype(jnp.float32) + tail).astype(jnp.bfloat16)


def shards(q, k, v, block_order, valid_frames, noise_steps, gate_table, out_weight, residual):
    tokens, width = q.shape[1:]
    ny = lax.axis_size(ROW)
    nx = lax.axis_size("span")
    rows = ny * tokens
    swap = [(0, 1), (1, 0)]
    vmem = pl.BlockSpec(memory_space=pltpu.VMEM)
    smem = pl.BlockSpec(memory_space=pltpu.SMEM)
    bf16 = jnp.bfloat16
    params = pltpu.CompilerParams(vmem_limit_bytes=48 * 1024 * 1024)

    def call(kernel, shapes, in_specs, name):
        shapes = [jax.ShapeDtypeStruct(shape, bf16) for shape in shapes]
        return pl.pallas_call(
            kernel,
            out_shape=shapes if len(shapes) > 1 else shapes[0],
            in_specs=in_specs,
            out_specs=[vmem] * len(shapes) if len(shapes) > 1 else vmem,
            compiler_params=params,
            name=name,
        )

    packed = call(pack_kernel, [(ny, 3, tokens, HD)], [vmem] * 3, "pack")(q[0], k[0], v[0])
    with jax.named_scope("exchange_heads"):
        packed = lax.all_to_all(packed, ROW, 0, 0, tiled=True)
    with jax.named_scope("gather_q"):
        queries = jnp.broadcast_to(packed[:, 0].reshape(1, rows, HD), (nx, rows, HD))
        queries = lax.all_to_all(queries, "span", 0, 0, tiled=True)
    with jax.named_scope("gather_kv"):
        kv = jnp.swapaxes(packed[:, 1:], 0, 1).reshape(2, rows, HD)
        kv_far = lax.ppermute(kv, "zh", swap)
        near = lax.all_gather(kv, "core", axis=0, tiled=True)
        far = lax.all_gather(kv_far, "core", axis=0, tiled=True)
    with jax.named_scope("fetch_weight"):
        weight = out_weight.T
        weight_far = lax.ppermute(weight, "y0", swap)
    parts = call(attend_kernel, [(nx, rows, 2 * HD)], [smem, smem, vmem, vmem, vmem], "attend")(
        block_order, valid_frames, queries, near, far
    )
    with jax.named_scope("return_parts"):
        parts = lax.all_to_all(parts, "span", 0, 0, tiled=True)
    near, send = call(combine_kernel, [(ny, rows // 2, HD), (2, rows // 2, HD)], [vmem], "combine")(parts)
    with jax.named_scope("gather_attended"):
        far = lax.ppermute(send, "zh", swap)
        near = lax.all_to_all(near, ROW, 0, 0, tiled=True)
        far = jnp.broadcast_to(far, (ny // 2,) + far.shape).reshape(ny, rows // 2, HD)
        far = lax.all_to_all(far, ROW, 0, 0, tiled=True)
        near, far = lax.optimization_barrier((near, far))
        near = lax.all_gather(near, "core", axis=0, tiled=True)
        far = lax.all_gather(far, "core", axis=0, tiled=True)
    cols = weight.shape[0]
    pieces = call(project_kernel, [(8, 4 * tokens * cols // HD, HD)], [vmem] * 4, "project")(
        near, far, weight, weight_far
    )
    with jax.named_scope("sum_heads"):
        pieces = lax.all_to_all(pieces, ("head", "y0"), 0, 0, tiled=True)
    mixed = pl.pallas_call(
        finish_kernel,
        out_shape=jax.ShapeDtypeStruct(residual.shape[:0:-1], bf16),
        in_specs=[smem, vmem, vmem, vmem],
        out_specs=vmem,
        compiler_params=params,
        name="finish",
    )(noise_steps, pieces, gate_table, residual[0].T)
    return mixed.T[None]


def solution(mesh):
    fine = Mesh(mesh.devices.reshape(4, 2, 2, 2, 2, 2, 4), AXES)
    seq = ("zh",) + ROW + ("core",)
    placed = (
        P("span", seq, "head"),
        P("span", seq, "head"),
        P("span", seq, "head"),
        P(),
        P(),
        P(),
        P(None, seq),
        P("head", seq),
        P("span", "head", seq),
    )
    return jax.shard_map(
        shards, mesh=fine, in_specs=placed, out_specs=P("span", "head", seq), check_vma=False
    )
```

```python
import math

import jax
import jax.numpy as jnp
from jax import lax
from jax.experimental import pallas as pl
from jax.experimental.pallas import tpu as pltpu
from jax.sharding import Mesh, PartitionSpec as P

HD = 128
CLOSED = -1e30
LOWEST = -1e20
AXES = ("span", "zh", "y2", "y1", "y0", "core", "head")
ROW = ("y2", "y1", "y0")
FRAME = ("zh", "y2", "y1")
FRAMES = 8


def pack_kernel(q_ref, k_ref, v_ref, out_ref):
    heads = q_ref.shape[1] // HD
    for h in range(out_ref.shape[0]):
        for i, ref in enumerate((q_ref, k_ref, v_ref)):
            if h < heads:
                out_ref[h, i] = ref[:, h * HD : (h + 1) * HD]
            else:
                out_ref[h, i] = jnp.zeros(out_ref.shape[2:], out_ref.dtype)


def unpack_kernel(packed_ref, queries_ref, kv_ref):
    for y in range(packed_ref.shape[0]):
        for i in range(queries_ref.shape[0]):
            queries_ref[i, y] = packed_ref[y, 0]
        for i in range(2):
            kv_ref[i, y] = packed_ref[y, 1 + i]


def attend_kernel(order_ref, valid_ref, q_ref, near_ref, far_ref, out_ref):
    blocks, rows = q_ref.shape[:2]
    zh = lax.axis_index("zh")
    span = lax.axis_index("span")
    keys = jnp.concatenate([ref[i] for ref in (near_ref, far_ref) for i in (0, 2)])
    values = jnp.concatenate([ref[i] for ref in (near_ref, far_ref) for i in (1, 3)])
    place = lax.broadcasted_iota(jnp.int32, (1, 4 * rows), 1)
    inner = place
    for i in range(1, 4):
        inner = jnp.where(place >= i * rows, place - i * rows, inner)
    half = FRAMES // 2
    frame_rows = rows // half
    near_limit = (valid_ref[span] - half * zh) * frame_rows
    far_limit = (valid_ref[span] - half * (1 - zh)) * frame_rows
    limit = jnp.where(place < 2 * rows, near_limit, far_limit)
    bias = jnp.where(inner < limit, 0.0, CLOSED)
    lane = lax.broadcasted_iota(jnp.int32, (rows, HD), 1)
    scale = math.log2(math.e) / HD**0.5
    for block in range(blocks):
        closed = jnp.where(order_ref[span] <= order_ref[block], 0.0, CLOSED)
        s = lax.dot_general(q_ref[block], keys, (((1,), (1,)), ((), ())), preferred_element_type=jnp.float32)
        s = s * scale + (bias + closed)
        top = jnp.maximum(jnp.max(s, axis=1, keepdims=True), LOWEST)
        top = top.astype(jnp.bfloat16).astype(jnp.float32)
        w = jnp.exp2(s - top)
        total = jnp.sum(w, axis=1, keepdims=True)
        acc = jnp.dot(w.astype(jnp.bfloat16), values, preferred_element_type=jnp.float32)
        coarse = total.astype(jnp.bfloat16).astype(jnp.float32)
        stats = jnp.where(lane == 0, top, jnp.where(lane == 1, coarse, total - coarse))
        out_ref[block, :, :HD] = acc.astype(jnp.bfloat16)
        out_ref[block, :, HD:] = stats.astype(jnp.bfloat16)


def combine_kernel(parts_ref, out_ref):
    stats = parts_ref[:, :, HD:].astype(jnp.float32)
    top = stats[:, :, 0:1]
    factor = jnp.exp2(top - jnp.max(top, axis=0, keepdims=True))
    denominator = jnp.sum(factor * (stats[:, :, 1:2] + stats[:, :, 2:3]), axis=0)
    summed = jnp.sum(factor * parts_ref[:, :, :HD].astype(jnp.float32), axis=0)
    done = summed / denominator
    tokens = done.shape[0] // FRAMES
    for y0 in range(2):
        piece = jnp.concatenate([done[(2 * i + y0) * tokens : (2 * i + y0 + 1) * tokens] for i in range(FRAMES // 2)])
        out_ref[y0] = piece.astype(jnp.bfloat16)


def spread_kernel(near_ref, far_ref, out_ref):
    for y in range(out_ref.shape[0]):
        out_ref[y, 0] = near_ref[y % 2]
        out_ref[y, 1] = far_ref[y % 2]


def project_kernel(rows_ref, near_ref, far_ref, out_ref):
    zh = lax.axis_index("zh")
    y0 = lax.axis_index("y0")
    heads = near_ref.shape[1] // HD
    rows = rows_ref.shape[2]
    quarter = rows // 4
    for side in range(2):
        left = [jnp.concatenate([rows_ref[c * heads + h, side] for h in range(heads)], axis=1) for c in range(2)]
        for turn, weight in enumerate((near_ref, far_ref)):
            first, second = [
                lax.dot_general(part, weight[...], (((1,), (1,)), ((), ())), preferred_element_type=jnp.float32)
                for part in left
            ]
            for y2 in range(2):
                a, b = 2 * y2 * quarter, (2 * y2 + 1) * quarter
                piece = jnp.concatenate(
                    [first[a : a + quarter], second[a : a + quarter], first[b : b + quarter], second[b : b + quarter]]
                )
                slot = (2 * (zh ^ side) + y2) * 2 + (y0 ^ turn)
                out_ref[slot, :rows, :] = piece[:, :HD].astype(jnp.bfloat16)
                tail = jnp.concatenate([piece[: rows // 2, HD:], piece[rows // 2 :, HD:]], axis=1)
                out_ref[slot, rows:, :] = tail.astype(jnp.bfloat16)


def finish_kernel(steps_ref, pieces_ref, gate_ref, residual_ref, out_ref):
    step = steps_ref[lax.axis_index("span")]
    gate = gate_ref[pl.ds(step, 1), :]
    rows = residual_ref.shape[1] // 2
    half = rows // 2
    sums = []
    for y0 in range(2):
        total = pieces_ref[y0].astype(jnp.float32)
        for head in range(1, 4):
            total = total + pieces_ref[2 * head + y0].astype(jnp.float32)
        sums.append(total)
    near, far = sums
    main = jnp.concatenate([near[:half], far[:half], near[half:rows], far[half:rows]])
    rest = HD // 2
    tail = jnp.concatenate([near[rows:, :rest], far[rows:, :rest], near[rows:, rest:], far[rows:, rest:]])
    main = (main * gate[:, :HD]).T
    tail = (tail * gate[:, HD:]).T
    out_ref[:HD, :] = (residual_ref[:HD, :].astype(jnp.float32) + main).astype(jnp.bfloat16)
    out_ref[HD:, :] = (residual_ref[HD:, :].astype(jnp.float32) + tail).astype(jnp.bfloat16)


def shards(q, k, v, block_order, valid_frames, noise_steps, gate_table, out_weight, residual):
    tokens, width = q.shape[1:]
    ny = lax.axis_size(ROW)
    nx = lax.axis_size("span")
    rows = ny * tokens
    swap = [(0, 1), (1, 0)]
    vmem = pl.BlockSpec(memory_space=pltpu.VMEM)
    smem = pl.BlockSpec(memory_space=pltpu.SMEM)
    bf16 = jnp.bfloat16
    params = pltpu.CompilerParams(vmem_limit_bytes=48 * 1024 * 1024)

    def call(kernel, shapes, in_specs, name):
        shapes = [jax.ShapeDtypeStruct(shape, bf16) for shape in shapes]
        return pl.pallas_call(
            kernel,
            out_shape=shapes if len(shapes) > 1 else shapes[0],
            in_specs=in_specs,
            out_specs=[vmem] * len(shapes) if len(shapes) > 1 else vmem,
            compiler_params=params,
            name=name,
        )

    packed = call(pack_kernel, [(ny, 3, tokens, HD)], [vmem] * 3, "pack")(q[0], k[0], v[0])
    with jax.named_scope("exchange_heads"):
        packed = lax.all_to_all(packed, ROW, 0, 0, tiled=True)
    queries, kv = call(unpack_kernel, [(nx, ny, tokens, HD), (2, ny, tokens, HD)], [vmem], "unpack")(packed)
    with jax.named_scope("gather_q"):
        queries = lax.all_to_all(queries.reshape(nx, rows, HD), "span", 0, 0, tiled=True)
    with jax.named_scope("gather_kv"):
        kv = kv.reshape(2, rows, HD)
        kv_far = lax.ppermute(kv, "zh", swap)
        near = lax.all_gather(kv, "core", axis=0, tiled=True)
        far = lax.all_gather(kv_far, "core", axis=0, tiled=True)
    with jax.named_scope("fetch_weight"):
        weight = out_weight.T
        weight_far = lax.ppermute(weight, "y0", swap)
    parts = call(attend_kernel, [(nx, rows, 2 * HD)], [smem, smem, vmem, vmem, vmem], "attend")(
        block_order, valid_frames, queries, near, far
    )
    with jax.named_scope("return_parts"):
        parts = lax.all_to_all(parts, "span", 0, 0, tiled=True)
    near = call(combine_kernel, [(2, rows // 2, HD)], [vmem], "combine")(parts)
    with jax.named_scope("gather_attended"):
        far = lax.ppermute(near, "zh", swap)
        both = call(spread_kernel, [(ny, 2, rows // 2, HD)], [vmem, vmem], "spread")(near, far)
        both = lax.all_to_all(both, ROW, 0, 0, tiled=True)[: width // HD]
        both = lax.all_gather(both, "core", axis=0, tiled=True)
    cols = weight.shape[0]
    pieces = call(project_kernel, [(8, 4 * tokens * cols // HD, HD)], [vmem] * 3, "project")(
        both, weight, weight_far
    )
    with jax.named_scope("sum_heads"):
        pieces = lax.all_to_all(pieces, ("head", "y0"), 0, 0, tiled=True)
    mixed = pl.pallas_call(
        finish_kernel,
        out_shape=jax.ShapeDtypeStruct(residual.shape[:0:-1], bf16),
        in_specs=[smem, vmem, vmem, vmem],
        out_specs=vmem,
        compiler_params=params,
        name="finish",
    )(noise_steps, pieces, gate_table, residual[0].T)
    return mixed.T[None]


def solution(mesh):
    fine = Mesh(mesh.devices.reshape(4, 2, 2, 2, 2, 2, 4), AXES)
    seq = ("zh",) + ROW + ("core",)
    placed = (
        P("span", seq, "head"),
        P("span", seq, "head"),
        P("span", seq, "head"),
        P(),
        P(),
        P(),
        P(None, seq),
        P("head", seq),
        P("span", "head", seq),
    )
    return jax.shard_map(
        shards, mesh=fine, in_specs=placed, out_specs=P("span", "head", seq), check_vma=False
    )
```

```python
import math

import jax
import jax.numpy as jnp
from jax import lax
from jax.experimental import pallas as pl
from jax.experimental.pallas import tpu as pltpu
from jax.sharding import Mesh, PartitionSpec as P

HD = 128
CLOSED = -1e30
LOWEST = -1e20
AXES = ("span", "zh", "y2", "y1", "y0", "core", "head")
ROW = ("y2", "y1", "y0")
FRAME = ("zh", "y2", "y1")
FRAMES = 8


def pack_kernel(q_ref, k_ref, v_ref, out_ref):
    heads = q_ref.shape[1] // HD
    for h in range(out_ref.shape[0]):
        for i, ref in enumerate((q_ref, k_ref, v_ref)):
            if h < heads:
                out_ref[h, i] = ref[:, h * HD : (h + 1) * HD]
            else:
                out_ref[h, i] = jnp.zeros(out_ref.shape[2:], out_ref.dtype)


def unpack_kernel(packed_ref, queries_ref, kv_ref):
    for y in range(packed_ref.shape[0]):
        for i in range(queries_ref.shape[0]):
            queries_ref[i, y] = packed_ref[y, 0]
        for i in range(2):
            kv_ref[i, y] = packed_ref[y, 1 + i]


def attend_kernel(order_ref, valid_ref, q_ref, near_ref, far_ref, out_ref):
    blocks, rows = q_ref.shape[:2]
    zh = lax.axis_index("zh")
    span = lax.axis_index("span")
    keys = jnp.concatenate([ref[i] for ref in (near_ref, far_ref) for i in (0, 2)])
    values = jnp.concatenate([ref[i] for ref in (near_ref, far_ref) for i in (1, 3)])
    place = lax.broadcasted_iota(jnp.int32, (1, 4 * rows), 1)
    inner = place
    for i in range(1, 4):
        inner = jnp.where(place >= i * rows, place - i * rows, inner)
    half = FRAMES // 2
    frame_rows = rows // half
    near_limit = (valid_ref[span] - half * zh) * frame_rows
    far_limit = (valid_ref[span] - half * (1 - zh)) * frame_rows
    limit = jnp.where(place < 2 * rows, near_limit, far_limit)
    bias = jnp.where(inner < limit, 0.0, CLOSED)
    lane = lax.broadcasted_iota(jnp.int32, (rows, HD), 1)
    scale = math.log2(math.e) / HD**0.5
    for block in range(blocks):
        closed = jnp.where(order_ref[span] <= order_ref[block], 0.0, CLOSED)
        s = lax.dot_general(q_ref[block], keys, (((1,), (1,)), ((), ())), preferred_element_type=jnp.float32)
        s = s * scale + (bias + closed)
        top = jnp.maximum(jnp.max(s, axis=1, keepdims=True), LOWEST)
        top = top.astype(jnp.bfloat16).astype(jnp.float32)
        w = jnp.exp2(s - top)
        total = jnp.sum(w, axis=1, keepdims=True)
        acc = jnp.dot(w.astype(jnp.bfloat16), values, preferred_element_type=jnp.float32)
        coarse = total.astype(jnp.bfloat16).astype(jnp.float32)
        stats = jnp.where(lane == 0, top, jnp.where(lane == 1, coarse, total - coarse))
        out_ref[block, :, :HD] = acc.astype(jnp.bfloat16)
        out_ref[block, :, HD:] = stats.astype(jnp.bfloat16)


def combine_kernel(parts_ref, out_ref):
    stats = parts_ref[:, :, HD:].astype(jnp.float32)
    top = stats[:, :, 0:1]
    factor = jnp.exp2(top - jnp.max(top, axis=0, keepdims=True))
    denominator = jnp.sum(factor * (stats[:, :, 1:2] + stats[:, :, 2:3]), axis=0)
    summed = jnp.sum(factor * parts_ref[:, :, :HD].astype(jnp.float32), axis=0)
    done = summed / denominator
    tokens = done.shape[0] // FRAMES
    places = out_ref.shape[0]
    for i in range(places):
        piece = jnp.concatenate([done[j * tokens : (j + 1) * tokens] for j in range(i, FRAMES, places)])
        out_ref[i] = piece.astype(jnp.bfloat16)


def spread_kernel(near_ref, far_ref, out_ref):
    for y in range(out_ref.shape[0]):
        place = y % near_ref.shape[0]
        out_ref[y, 0] = near_ref[place]
        out_ref[y, 1] = far_ref[place]


def project_kernel(rows_ref, weights_ref, out_ref):
    zh = lax.axis_index("zh")
    heads = weights_ref.shape[2] // HD
    rows = rows_ref.shape[2]
    half = rows // 2
    left = jnp.concatenate(
        [
            jnp.concatenate([rows_ref[c * heads + h, side] for h in range(heads)], axis=1)
            for side in range(2)
            for c in range(2)
        ]
    )
    places = weights_ref.shape[0]
    for place in range(places):
        product = lax.dot_general(
            left, weights_ref[place], (((1,), (1,)), ((), ())), preferred_element_type=jnp.float32
        )
        for side in range(2):
            for y2 in range(2):
                a = 2 * side * rows + y2 * half
                first, second = product[a : a + half], product[a + rows : a + rows + half]
                slot = (2 * (zh ^ side) + y2) * places + place
                main = jnp.concatenate([first[:, :HD], second[:, :HD]])
                out_ref[slot, :rows, :] = main.astype(jnp.bfloat16)
                tail = jnp.concatenate([first[:, HD:], second[:, HD:]], axis=1)
                out_ref[slot, rows:, :] = tail.astype(jnp.bfloat16)


def finish_kernel(steps_ref, pieces_ref, gate_ref, residual_ref, out_ref):
    step = steps_ref[lax.axis_index("span")]
    gate = gate_ref[pl.ds(step, 1), :]
    places = pieces_ref.shape[0] // 4
    rows = residual_ref.shape[1] // places
    rest = HD // 2
    mains, tails = [], []
    for place in range(places):
        total = pieces_ref[place].astype(jnp.float32)
        for head in range(1, 4):
            total = total + pieces_ref[places * head + place].astype(jnp.float32)
        mains.append(total[:rows])
        tails += [total[rows:, :rest], total[rows:, rest:]]
    main = (jnp.concatenate(mains) * gate[:, :HD]).T
    tail = (jnp.concatenate(tails) * gate[:, HD:]).T
    out_ref[:HD, :] = (residual_ref[:HD, :].astype(jnp.float32) + main).astype(jnp.bfloat16)
    out_ref[HD:, :] = (residual_ref[HD:, :].astype(jnp.float32) + tail).astype(jnp.bfloat16)


def shards(q, k, v, block_order, valid_frames, noise_steps, gate_table, out_weight, residual):
    tokens, width = q.shape[1:]
    ny = lax.axis_size(ROW)
    nx = lax.axis_size("span")
    rows = ny * tokens
    swap = [(0, 1), (1, 0)]
    vmem = pl.BlockSpec(memory_space=pltpu.VMEM)
    smem = pl.BlockSpec(memory_space=pltpu.SMEM)
    bf16 = jnp.bfloat16
    params = pltpu.CompilerParams(vmem_limit_bytes=48 * 1024 * 1024)

    def call(kernel, shapes, in_specs, name):
        shapes = [jax.ShapeDtypeStruct(shape, bf16) for shape in shapes]
        return pl.pallas_call(
            kernel,
            out_shape=shapes if len(shapes) > 1 else shapes[0],
            in_specs=in_specs,
            out_specs=[vmem] * len(shapes) if len(shapes) > 1 else vmem,
            compiler_params=params,
            name=name,
        )

    packed = call(pack_kernel, [(ny, 3, tokens, HD)], [vmem] * 3, "pack")(q[0], k[0], v[0])
    with jax.named_scope("exchange_heads"):
        packed = lax.all_to_all(packed, ROW, 0, 0, tiled=True)
    queries, kv = call(unpack_kernel, [(nx, ny, tokens, HD), (2, ny, tokens, HD)], [vmem], "unpack")(packed)
    with jax.named_scope("gather_q"):
        queries = lax.all_to_all(queries.reshape(nx, rows, HD), "span", 0, 0, tiled=True)
    with jax.named_scope("gather_kv"):
        kv = kv.reshape(2, rows, HD)
        kv_far = lax.ppermute(kv, "zh", swap)
        near = lax.all_gather(kv, "core", axis=0, tiled=True)
        far = lax.all_gather(kv_far, "core", axis=0, tiled=True)
    with jax.named_scope("fetch_weight"):
        weight, kv = lax.optimization_barrier((out_weight.T, kv))
        weights = lax.all_gather(weight, ("y1", "y0"), axis=0, tiled=False)
    parts = call(attend_kernel, [(nx, rows, 2 * HD)], [smem, smem, vmem, vmem, vmem], "attend")(
        block_order, valid_frames, queries, near, far
    )
    with jax.named_scope("return_parts"):
        parts = lax.all_to_all(parts, "span", 0, 0, tiled=True)
    near = call(combine_kernel, [(4, rows // 4, HD)], [vmem], "combine")(parts)
    with jax.named_scope("gather_attended"):
        far = lax.ppermute(near, "zh", swap)
        both = call(spread_kernel, [(ny, 2, rows // 4, HD)], [vmem, vmem], "spread")(near, far)
        both = lax.all_to_all(both, ROW, 0, 0, tiled=True)[: width // HD]
        both = lax.all_gather(both, "core", axis=0, tiled=True)
    cols = weight.shape[0]
    pieces = call(project_kernel, [(16, 2 * tokens * cols // HD, HD)], [vmem] * 2, "project")(both, weights)
    with jax.named_scope("sum_heads"):
        pieces = lax.all_to_all(pieces, ("head", "y1", "y0"), 0, 0, tiled=True)
    mixed = pl.pallas_call(
        finish_kernel,
        out_shape=jax.ShapeDtypeStruct(residual.shape[:0:-1], bf16),
        in_specs=[smem, vmem, vmem, vmem],
        out_specs=vmem,
        compiler_params=params,
        name="finish",
    )(noise_steps, pieces, gate_table, residual[0].T)
    return mixed.T[None]


def solution(mesh):
    fine = Mesh(mesh.devices.reshape(4, 2, 2, 2, 2, 2, 4), AXES)
    seq = ("zh",) + ROW + ("core",)
    placed = (
        P("span", seq, "head"),
        P("span", seq, "head"),
        P("span", seq, "head"),
        P(),
        P(),
        P(),
        P(None, seq),
        P("head", seq),
        P("span", "head", seq),
    )
    return jax.shard_map(
        shards, mesh=fine, in_specs=placed, out_specs=P("span", "head", seq), check_vma=False
    )
```

```python
import math

import jax
import jax.numpy as jnp
from jax import lax
from jax.experimental import pallas as pl
from jax.experimental.pallas import tpu as pltpu
from jax.sharding import Mesh, PartitionSpec as P

HD = 128
CLOSED = -1e30
LOWEST = -1e20
AXES = ("span", "zh", "y2", "y1", "y0", "core", "head")
ROW = ("y2", "y1", "y0")
FRAME = ("zh", "y2", "y1")
FRAMES = 8


def pack_kernel(q_ref, k_ref, v_ref, out_ref):
    heads = q_ref.shape[1] // HD
    for h in range(out_ref.shape[0]):
        for i, ref in enumerate((q_ref, k_ref, v_ref)):
            if h < heads:
                out_ref[h, i] = ref[:, h * HD : (h + 1) * HD]
            else:
                out_ref[h, i] = jnp.zeros(out_ref.shape[2:], out_ref.dtype)


def unpack_kernel(packed_ref, queries_ref, kv_ref):
    for y in range(packed_ref.shape[0]):
        for i in range(queries_ref.shape[0]):
            queries_ref[i, y] = packed_ref[y, 0]
        for i in range(2):
            kv_ref[i, y] = packed_ref[y, 1 + i]


def attend_kernel(order_ref, valid_ref, q_ref, near_ref, far_ref, out_ref):
    blocks, rows = q_ref.shape[:2]
    zh = lax.axis_index("zh")
    span = lax.axis_index("span")
    keys = jnp.concatenate([ref[i] for ref in (near_ref, far_ref) for i in (0, 2)])
    values = jnp.concatenate([ref[i] for ref in (near_ref, far_ref) for i in (1, 3)])
    place = lax.broadcasted_iota(jnp.int32, (1, 4 * rows), 1)
    inner = place
    for i in range(1, 4):
        inner = jnp.where(place >= i * rows, place - i * rows, inner)
    half = FRAMES // 2
    frame_rows = rows // half
    near_limit = (valid_ref[span] - half * zh) * frame_rows
    far_limit = (valid_ref[span] - half * (1 - zh)) * frame_rows
    limit = jnp.where(place < 2 * rows, near_limit, far_limit)
    bias = jnp.where(inner < limit, 0.0, CLOSED)
    lane = lax.broadcasted_iota(jnp.int32, (rows, HD), 1)
    scale = math.log2(math.e) / HD**0.5
    for block in range(blocks):
        closed = jnp.where(order_ref[span] <= order_ref[block], 0.0, CLOSED)
        s = lax.dot_general(q_ref[block], keys, (((1,), (1,)), ((), ())), preferred_element_type=jnp.float32)
        s = s * scale + (bias + closed)
        top = jnp.maximum(jnp.max(s, axis=1, keepdims=True), LOWEST)
        top = top.astype(jnp.bfloat16).astype(jnp.float32)
        w = jnp.exp2(s - top)
        total = jnp.sum(w, axis=1, keepdims=True)
        acc = jnp.dot(w.astype(jnp.bfloat16), values, preferred_element_type=jnp.float32)
        coarse = total.astype(jnp.bfloat16).astype(jnp.float32)
        stats = jnp.where(lane == 0, top, jnp.where(lane == 1, coarse, total - coarse))
        out_ref[block, :, :HD] = acc.astype(jnp.bfloat16)
        out_ref[block, :, HD:] = stats.astype(jnp.bfloat16)


def combine_kernel(parts_ref, out_ref):
    stats = parts_ref[:, :, HD:].astype(jnp.float32)
    top = stats[:, :, 0:1]
    factor = jnp.exp2(top - jnp.max(top, axis=0, keepdims=True))
    denominator = jnp.sum(factor * (stats[:, :, 1:2] + stats[:, :, 2:3]), axis=0)
    summed = jnp.sum(factor * parts_ref[:, :, :HD].astype(jnp.float32), axis=0)
    done = summed / denominator
    tokens = done.shape[0] // FRAMES
    for y0 in range(2):
        piece = jnp.concatenate([done[(2 * i + y0) * tokens : (2 * i + y0 + 1) * tokens] for i in range(FRAMES // 2)])
        out_ref[y0] = piece.astype(jnp.bfloat16)


def spread_kernel(near_ref, far_ref, out_ref):
    for y in range(out_ref.shape[0]):
        out_ref[y, 0] = near_ref[y % 2]
        out_ref[y, 1] = far_ref[y % 2]


def project_kernel(rows_ref, near_ref, far_ref, out_ref):
    zh = lax.axis_index("zh")
    y0 = lax.axis_index("y0")
    heads = near_ref.shape[1] // HD
    rows = rows_ref.shape[2]
    quarter = rows // 4
    for side in range(2):
        left = [jnp.concatenate([rows_ref[c * heads + h, side] for h in range(heads)], axis=1) for c in range(2)]
        for turn, weight in enumerate((near_ref, far_ref)):
            first, second = [
                lax.dot_general(part, weight[...], (((1,), (1,)), ((), ())), preferred_element_type=jnp.float32)
                for part in left
            ]
            for y2 in range(2):
                a, b = 2 * y2 * quarter, (2 * y2 + 1) * quarter
                piece = jnp.concatenate(
                    [first[a : a + quarter], second[a : a + quarter], first[b : b + quarter], second[b : b + quarter]]
                )
                slot = (2 * (zh ^ side) + y2) * 2 + (y0 ^ turn)
                out_ref[slot, :rows, :] = piece[:, :HD].astype(jnp.bfloat16)
                tail = jnp.concatenate([piece[: rows // 2, HD:], piece[rows // 2 :, HD:]], axis=1)
                out_ref[slot, rows:, :] = tail.astype(jnp.bfloat16)


def finish_kernel(steps_ref, pieces_ref, gate_ref, residual_ref, out_ref):
    step = steps_ref[lax.axis_index("span")]
    gate = gate_ref[pl.ds(step, 1), :]
    rows = residual_ref.shape[1] // 2
    half = rows // 2
    sums = []
    for y0 in range(2):
        total = pieces_ref[y0].astype(jnp.float32)
        for head in range(1, 4):
            total = total + pieces_ref[2 * head + y0].astype(jnp.float32)
        sums.append(total)
    near, far = sums
    main = jnp.concatenate([near[:half], far[:half], near[half:rows], far[half:rows]])
    rest = HD // 2
    tail = jnp.concatenate([near[rows:, :rest], far[rows:, :rest], near[rows:, rest:], far[rows:, rest:]])
    main = (main * gate[:, :HD]).T
    tail = (tail * gate[:, HD:]).T
    out_ref[:HD, :] = (residual_ref[:HD, :].astype(jnp.float32) + main).astype(jnp.bfloat16)
    out_ref[HD:, :] = (residual_ref[HD:, :].astype(jnp.float32) + tail).astype(jnp.bfloat16)


def shards(q, k, v, block_order, valid_frames, noise_steps, gate_table, out_weight, residual):
    tokens, width = q.shape[1:]
    ny = lax.axis_size(ROW)
    nx = lax.axis_size("span")
    rows = ny * tokens
    swap = [(0, 1), (1, 0)]
    vmem = pl.BlockSpec(memory_space=pltpu.VMEM)
    smem = pl.BlockSpec(memory_space=pltpu.SMEM)
    bf16 = jnp.bfloat16
    params = pltpu.CompilerParams(vmem_limit_bytes=48 * 1024 * 1024)

    def call(kernel, shapes, in_specs, name):
        shapes = [jax.ShapeDtypeStruct(shape, bf16) for shape in shapes]
        return pl.pallas_call(
            kernel,
            out_shape=shapes if len(shapes) > 1 else shapes[0],
            in_specs=in_specs,
            out_specs=[vmem] * len(shapes) if len(shapes) > 1 else vmem,
            compiler_params=params,
            name=name,
        )

    packed = call(pack_kernel, [(ny, 3, tokens, HD)], [vmem] * 3, "pack")(q[0], k[0], v[0])
    with jax.named_scope("exchange_heads"):
        packed = lax.all_to_all(packed, ROW, 0, 0, tiled=True)
    queries, kv = call(unpack_kernel, [(nx, ny, tokens, HD), (2, ny, tokens, HD)], [vmem], "unpack")(packed)
    with jax.named_scope("gather_q"):
        queries = lax.all_to_all(queries.reshape(nx, rows, HD), "span", 0, 0, tiled=True)
    with jax.named_scope("gather_kv"):
        kv = kv.reshape(2, rows, HD)
        kv_far = lax.ppermute(kv, "zh", swap)
        near = lax.all_gather(kv, "core", axis=0, tiled=True)
        far = lax.all_gather(kv_far, "core", axis=0, tiled=True)
    with jax.named_scope("fetch_weight"):
        weight, near = lax.optimization_barrier((out_weight.T, near))
        weight_far = lax.ppermute(weight, "y0", swap)
    parts = call(attend_kernel, [(nx, rows, 2 * HD)], [smem, smem, vmem, vmem, vmem], "attend")(
        block_order, valid_frames, queries, near, far
    )
    with jax.named_scope("return_parts"):
        parts = lax.all_to_all(parts, "span", 0, 0, tiled=True)
        parts, weight_far = lax.optimization_barrier((parts, weight_far))
    near = call(combine_kernel, [(2, rows // 2, HD)], [vmem], "combine")(parts)
    with jax.named_scope("gather_attended"):
        far = lax.ppermute(near, "zh", swap)
        both = call(spread_kernel, [(ny, 2, rows // 2, HD)], [vmem, vmem], "spread")(near, far)
        both = lax.all_to_all(both, ROW, 0, 0, tiled=True)[: width // HD]
        both = lax.all_gather(both, "core", axis=0, tiled=True)
    cols = weight.shape[0]
    pieces = call(project_kernel, [(8, 4 * tokens * cols // HD, HD)], [vmem] * 3, "project")(
        both, weight, weight_far
    )
    with jax.named_scope("sum_heads"):
        pieces = lax.all_to_all(pieces, ("head", "y0"), 0, 0, tiled=True)
    mixed = pl.pallas_call(
        finish_kernel,
        out_shape=jax.ShapeDtypeStruct(residual.shape[:0:-1], bf16),
        in_specs=[smem, vmem, vmem, vmem],
        out_specs=vmem,
        compiler_params=params,
        name="finish",
    )(noise_steps, pieces, gate_table, residual[0].T)
    return mixed.T[None]


def solution(mesh):
    fine = Mesh(mesh.devices.reshape(4, 2, 2, 2, 2, 2, 4), AXES)
    seq = ("zh",) + ROW + ("core",)
    placed = (
        P("span", seq, "head"),
        P("span", seq, "head"),
        P("span", seq, "head"),
        P(),
        P(),
        P(),
        P(None, seq),
        P("head", seq),
        P("span", "head", seq),
    )
    return jax.shard_map(
        shards, mesh=fine, in_specs=placed, out_specs=P("span", "head", seq), check_vma=False
    )
```

```python
import math

import jax
import jax.numpy as jnp
from jax import lax
from jax.experimental import pallas as pl
from jax.experimental.pallas import tpu as pltpu
from jax.sharding import Mesh, PartitionSpec as P

HD = 128
CLOSED = -1e30
LOWEST = -1e20
AXES = ("span", "zh", "y2", "y1", "y0", "core", "head")
ROW = ("y2", "y1", "y0")
FRAME = ("zh", "y2", "y1")
FRAMES = 8


def pack_kernel(q_ref, k_ref, v_ref, out_ref):
    heads = q_ref.shape[1] // HD
    for h in range(out_ref.shape[0]):
        for i, ref in enumerate((q_ref, k_ref, v_ref)):
            if h < heads:
                out_ref[h, i] = ref[:, h * HD : (h + 1) * HD]
            else:
                out_ref[h, i] = jnp.zeros(out_ref.shape[2:], out_ref.dtype)


def keep_kv_kernel(packed_ref, kv_ref):
    for y in range(packed_ref.shape[0]):
        for i in range(2):
            kv_ref[i, y] = packed_ref[y, 1 + i]


def repeat_q_kernel(packed_ref, queries_ref):
    for y in range(packed_ref.shape[0]):
        for i in range(queries_ref.shape[0]):
            queries_ref[i, y] = packed_ref[y, 0]


def attend_kernel(order_ref, valid_ref, q_ref, near_ref, far_ref, out_ref):
    blocks, rows = q_ref.shape[:2]
    zh = lax.axis_index("zh")
    span = lax.axis_index("span")
    keys = jnp.concatenate([ref[i] for ref in (near_ref, far_ref) for i in (0, 2)])
    values = jnp.concatenate([ref[i] for ref in (near_ref, far_ref) for i in (1, 3)])
    place = lax.broadcasted_iota(jnp.int32, (1, 4 * rows), 1)
    inner = place
    for i in range(1, 4):
        inner = jnp.where(place >= i * rows, place - i * rows, inner)
    half = FRAMES // 2
    frame_rows = rows // half
    near_limit = (valid_ref[span] - half * zh) * frame_rows
    far_limit = (valid_ref[span] - half * (1 - zh)) * frame_rows
    limit = jnp.where(place < 2 * rows, near_limit, far_limit)
    bias = jnp.where(inner < limit, 0.0, CLOSED)
    lane = lax.broadcasted_iota(jnp.int32, (rows, HD), 1)
    scale = math.log2(math.e) / HD**0.5
    for block in range(blocks):
        closed = jnp.where(order_ref[span] <= order_ref[block], 0.0, CLOSED)
        s = lax.dot_general(q_ref[block], keys, (((1,), (1,)), ((), ())), preferred_element_type=jnp.float32)
        s = s * scale + (bias + closed)
        top = jnp.maximum(jnp.max(s, axis=1, keepdims=True), LOWEST)
        top = top.astype(jnp.bfloat16).astype(jnp.float32)
        w = jnp.exp2(s - top)
        total = jnp.sum(w, axis=1, keepdims=True)
        acc = jnp.dot(w.astype(jnp.bfloat16), values, preferred_element_type=jnp.float32)
        coarse = total.astype(jnp.bfloat16).astype(jnp.float32)
        stats = jnp.where(lane == 0, top, jnp.where(lane == 1, coarse, total - coarse))
        out_ref[block, :, :HD] = acc.astype(jnp.bfloat16)
        out_ref[block, :, HD:] = stats.astype(jnp.bfloat16)


def combine_kernel(parts_ref, out_ref):
    stats = parts_ref[:, :, HD:].astype(jnp.float32)
    top = stats[:, :, 0:1]
    factor = jnp.exp2(top - jnp.max(top, axis=0, keepdims=True))
    denominator = jnp.sum(factor * (stats[:, :, 1:2] + stats[:, :, 2:3]), axis=0)
    summed = jnp.sum(factor * parts_ref[:, :, :HD].astype(jnp.float32), axis=0)
    done = summed / denominator
    tokens = done.shape[0] // FRAMES
    places = out_ref.shape[0]
    for i in range(places):
        piece = jnp.concatenate([done[j * tokens : (j + 1) * tokens] for j in range(i, FRAMES, places)])
        out_ref[i] = piece.astype(jnp.bfloat16)


def spread_kernel(near_ref, far_ref, out_ref):
    for y in range(out_ref.shape[0]):
        place = y % near_ref.shape[0]
        out_ref[y, 0] = near_ref[place]
        out_ref[y, 1] = far_ref[place]


def project_kernel(rows_ref, near_ref, far_ref, out_ref):
    zh = lax.axis_index("zh")
    mine = 2 * lax.axis_index("y1") + lax.axis_index("y0")
    heads = near_ref.shape[2] // HD
    rows = rows_ref.shape[2]
    slots = rows_ref.shape[0] // 2
    half = rows // 2
    left = jnp.concatenate(
        [
            jnp.concatenate([rows_ref[c * slots + h, side] for h in range(heads)], axis=1)
            for side in range(2)
            for c in range(2)
        ]
    )
    places = 4
    for turn in range(places):
        weight = (far_ref if turn > 1 else near_ref)[turn % 2]
        product = lax.dot_general(
            left, weight, (((1,), (1,)), ((), ())), preferred_element_type=jnp.float32
        )
        for side in range(2):
            for y2 in range(2):
                a = 2 * side * rows + y2 * half
                first, second = product[a : a + half], product[a + rows : a + rows + half]
                slot = (2 * (zh ^ side) + y2) * places + (mine ^ turn)
                main = jnp.concatenate([first[:, :HD], second[:, :HD]])
                out_ref[slot, :rows, :] = main.astype(jnp.bfloat16)
                tail = jnp.concatenate([first[:, HD:], second[:, HD:]], axis=1)
                out_ref[slot, rows:, :] = tail.astype(jnp.bfloat16)


def finish_kernel(steps_ref, pieces_ref, gate_ref, residual_ref, out_ref):
    step = steps_ref[lax.axis_index("span")]
    gate = gate_ref[pl.ds(step, 1), :]
    places = pieces_ref.shape[0] // 4
    rows = residual_ref.shape[1] // places
    rest = HD // 2
    mains, tails = [], []
    for place in range(places):
        total = pieces_ref[place].astype(jnp.float32)
        for head in range(1, 4):
            total = total + pieces_ref[places * head + place].astype(jnp.float32)
        mains.append(total[:rows])
        tails += [total[rows:, :rest], total[rows:, rest:]]
    main = (jnp.concatenate(mains) * gate[:, :HD]).T
    tail = (jnp.concatenate(tails) * gate[:, HD:]).T
    out_ref[:HD, :] = (residual_ref[:HD, :].astype(jnp.float32) + main).astype(jnp.bfloat16)
    out_ref[HD:, :] = (residual_ref[HD:, :].astype(jnp.float32) + tail).astype(jnp.bfloat16)


def shards(q, k, v, block_order, valid_frames, noise_steps, gate_table, out_weight, residual):
    tokens, width = q.shape[1:]
    ny = lax.axis_size(ROW)
    nx = lax.axis_size("span")
    rows = ny * tokens
    swap = [(0, 1), (1, 0)]
    vmem = pl.BlockSpec(memory_space=pltpu.VMEM)
    smem = pl.BlockSpec(memory_space=pltpu.SMEM)
    bf16 = jnp.bfloat16
    params = pltpu.CompilerParams(vmem_limit_bytes=48 * 1024 * 1024)

    def call(kernel, shapes, in_specs, name):
        shapes = [jax.ShapeDtypeStruct(shape, bf16) for shape in shapes]
        return pl.pallas_call(
            kernel,
            out_shape=shapes if len(shapes) > 1 else shapes[0],
            in_specs=in_specs,
            out_specs=[vmem] * len(shapes) if len(shapes) > 1 else vmem,
            compiler_params=params,
            name=name,
        )

    packed = call(pack_kernel, [(ny, 3, tokens, HD)], [vmem] * 3, "pack")(q[0], k[0], v[0])
    with jax.named_scope("exchange_heads"):
        packed = lax.all_to_all(packed, ROW, 0, 0, tiled=True)
    with jax.named_scope("gather_kv"):
        kv = call(keep_kv_kernel, [(2, ny, tokens, HD)], [vmem], "keep_kv")(packed).reshape(2, rows, HD)
        kv_far = lax.ppermute(kv, "zh", swap)
    with jax.named_scope("gather_q"):
        packed, kv = lax.optimization_barrier((packed, kv))
        queries = call(repeat_q_kernel, [(nx, ny, tokens, HD)], [vmem], "repeat_q")(packed)
        queries = lax.all_to_all(queries.reshape(nx, rows, HD), "span", 0, 0, tiled=True)
    with jax.named_scope("gather_kv"):
        near = lax.all_gather(kv, "core", axis=0, tiled=True)
        far = lax.all_gather(kv_far, "core", axis=0, tiled=True)
    with jax.named_scope("fetch_weight"):
        weight = out_weight.T
        weights = jnp.stack([weight, lax.ppermute(weight, "y0", swap)])
        weights_far = lax.ppermute(weights, "y1", swap)
    parts = call(attend_kernel, [(nx, rows, 2 * HD)], [smem, smem, vmem, vmem, vmem], "attend")(
        block_order, valid_frames, queries, near, far
    )
    with jax.named_scope("return_parts"):
        parts = lax.all_to_all(parts, "span", 0, 0, tiled=True)
    near = call(combine_kernel, [(4, rows // 4, HD)], [vmem], "combine")(parts)
    with jax.named_scope("gather_attended"):
        far = lax.ppermute(near, "zh", swap)
        far, weights_far = lax.optimization_barrier((far, weights_far))
        both = call(spread_kernel, [(ny, 2, rows // 4, HD)], [vmem, vmem], "spread")(near, far)
        both = lax.all_to_all(both, ROW, 0, 0, tiled=True)
        both = lax.all_gather(both, "core", axis=0, tiled=True)
    cols = weight.shape[0]
    pieces = call(project_kernel, [(16, 2 * tokens * cols // HD, HD)], [vmem] * 3, "project")(
        both, weights, weights_far
    )
    with jax.named_scope("sum_heads"):
        pieces = lax.all_to_all(pieces, ("head", "y1", "y0"), 0, 0, tiled=True)
    mixed = pl.pallas_call(
        finish_kernel,
        out_shape=jax.ShapeDtypeStruct(residual.shape[:0:-1], bf16),
        in_specs=[smem, vmem, vmem, vmem],
        out_specs=vmem,
        compiler_params=params,
        name="finish",
    )(noise_steps, pieces, gate_table, residual[0].T)
    return mixed.T[None]


def solution(mesh):
    fine = Mesh(mesh.devices.reshape(4, 2, 2, 2, 2, 2, 4), AXES)
    seq = ("zh",) + ROW + ("core",)
    placed = (
        P("span", seq, "head"),
        P("span", seq, "head"),
        P("span", seq, "head"),
        P(),
        P(),
        P(),
        P(None, seq),
        P("head", seq),
        P("span", "head", seq),
    )
    return jax.shard_map(
        shards, mesh=fine, in_specs=placed, out_specs=P("span", "head", seq), check_vma=False
    )
```

```python
import functools
import math

import jax
import jax.numpy as jnp
from jax import lax
from jax.experimental import pallas as pl
from jax.experimental.pallas import tpu as pltpu
from jax.sharding import Mesh, PartitionSpec as P

HD = 128
CLOSED = -1e30
LOWEST = -1e20
SPACE = 16
AXES = ("span", "zh", "y2", "y1", "y0", "core", "head")
ROW = ("y2", "y1", "y0")
FRAME = ("zh", "y2", "y1")
FRAMES = 8


def pack_kernel(q_ref, k_ref, v_ref, out_ref):
    heads = q_ref.shape[1] // HD
    for h in range(out_ref.shape[0]):
        for i, ref in enumerate((q_ref, k_ref, v_ref)):
            if h < heads:
                out_ref[h, i] = ref[:, h * HD : (h + 1) * HD]
            else:
                out_ref[h, i] = jnp.zeros(out_ref.shape[2:], out_ref.dtype)


def keep_kv_kernel(packed_ref, kv_ref):
    for y in range(packed_ref.shape[0]):
        for i in range(2):
            kv_ref[i, y] = packed_ref[y, 1 + i]


def repeat_q_kernel(packed_ref, queries_ref):
    for y in range(packed_ref.shape[0]):
        for i in range(queries_ref.shape[0]):
            queries_ref[i, y] = packed_ref[y, 0]


def attend_kernel(order_ref, valid_ref, q_ref, near_ref, far_ref, out_ref):
    blocks, rows = q_ref.shape[:2]
    zh = lax.axis_index("zh")
    span = lax.axis_index("span")
    keys = jnp.concatenate([ref[i] for ref in (near_ref, far_ref) for i in (0, 2)])
    values = jnp.concatenate([ref[i] for ref in (near_ref, far_ref) for i in (1, 3)])
    place = lax.broadcasted_iota(jnp.int32, (1, 4 * rows), 1)
    inner = place
    for i in range(1, 4):
        inner = jnp.where(place >= i * rows, place - i * rows, inner)
    half = FRAMES // 2
    frame_rows = rows // half
    near_limit = (valid_ref[span] - half * zh) * frame_rows
    far_limit = (valid_ref[span] - half * (1 - zh)) * frame_rows
    limit = jnp.where(place < 2 * rows, near_limit, far_limit)
    bias = jnp.where(inner < limit, 0.0, CLOSED)
    lane = lax.broadcasted_iota(jnp.int32, (rows, HD), 1)
    stats = jnp.zeros((rows, HD), jnp.float32)
    scale = math.log2(math.e) / HD**0.5
    for block in range(blocks):
        closed = jnp.where(order_ref[span] <= order_ref[block], 0.0, CLOSED)
        s = lax.dot_general(q_ref[block], keys, (((1,), (1,)), ((), ())), preferred_element_type=jnp.float32)
        s = s * scale + (bias + closed)
        top = jnp.maximum(jnp.max(s, axis=1, keepdims=True), LOWEST)
        top = top.astype(jnp.bfloat16).astype(jnp.float32)
        w = jnp.exp2(s - top)
        total = jnp.sum(w, axis=1, keepdims=True)
        acc = jnp.dot(w.astype(jnp.bfloat16), values, preferred_element_type=jnp.float32)
        out_ref[block, :rows, :] = acc.astype(jnp.bfloat16)
        coarse = total.astype(jnp.bfloat16).astype(jnp.float32)
        stats = jnp.where(lane == SPACE * block, top, stats)
        stats = jnp.where(lane == SPACE * block + 1, coarse, stats)
        stats = jnp.where(lane == SPACE * block + 2, total - coarse, stats)
    places = out_ref.shape[1] - rows
    wide = jnp.concatenate([stats, jnp.zeros((places // SPACE * HD - rows, HD), jnp.float32)]).T
    wide = wide.astype(jnp.bfloat16)
    for block in range(blocks):
        for i in range(places // SPACE):
            piece = wide[SPACE * block : SPACE * (block + 1), i * HD : (i + 1) * HD]
            out_ref[block, rows + SPACE * i : rows + SPACE * (i + 1), :] = piece


def combine_kernel(parts_ref, out_ref):
    blocks = parts_ref.shape[0]
    rows = out_ref.shape[0] * out_ref.shape[1]
    count = (parts_ref.shape[1] - rows) // SPACE
    wide = jnp.concatenate(
        [
            jnp.concatenate([parts_ref[b, rows + SPACE * i : rows + SPACE * (i + 1), :] for i in range(count)], axis=1)
            for b in range(blocks)
        ]
    )
    stats = wide.astype(jnp.float32).T[:rows]
    tops = [stats[:, SPACE * b : SPACE * b + 1] for b in range(blocks)]
    highest = functools.reduce(jnp.maximum, tops)
    denominator, summed = 0.0, 0.0
    for b in range(blocks):
        factor = jnp.exp2(tops[b] - highest)
        place = SPACE * b
        denominator = denominator + factor * (stats[:, place + 1 : place + 2] + stats[:, place + 2 : place + 3])
        summed = summed + factor * parts_ref[b, :rows, :].astype(jnp.float32)
    done = summed / denominator
    tokens = done.shape[0] // FRAMES
    for y0 in range(2):
        piece = jnp.concatenate([done[(2 * i + y0) * tokens : (2 * i + y0 + 1) * tokens] for i in range(FRAMES // 2)])
        out_ref[y0] = piece.astype(jnp.bfloat16)


def spread_kernel(near_ref, far_ref, out_ref):
    for y in range(out_ref.shape[0]):
        out_ref[y, 0] = near_ref[y % 2]
        out_ref[y, 1] = far_ref[y % 2]


def project_kernel(rows_ref, near_ref, far_ref, out_ref):
    zh = lax.axis_index("zh")
    y0 = lax.axis_index("y0")
    heads = near_ref.shape[1] // HD
    rows = rows_ref.shape[2]
    quarter = rows // 4
    for side in range(2):
        left = [jnp.concatenate([rows_ref[c * heads + h, side] for h in range(heads)], axis=1) for c in range(2)]
        for turn, weight in enumerate((near_ref, far_ref)):
            first, second = [
                lax.dot_general(part, weight[...], (((1,), (1,)), ((), ())), preferred_element_type=jnp.float32)
                for part in left
            ]
            for y2 in range(2):
                a, b = 2 * y2 * quarter, (2 * y2 + 1) * quarter
                piece = jnp.concatenate(
                    [first[a : a + quarter], second[a : a + quarter], first[b : b + quarter], second[b : b + quarter]]
                )
                slot = (2 * (zh ^ side) + y2) * 2 + (y0 ^ turn)
                out_ref[slot, :rows, :] = piece[:, :HD].astype(jnp.bfloat16)
                tail = jnp.concatenate([piece[: rows // 2, HD:], piece[rows // 2 :, HD:]], axis=1)
                out_ref[slot, rows:, :] = tail.astype(jnp.bfloat16)


def finish_kernel(steps_ref, pieces_ref, gate_ref, residual_ref, out_ref):
    step = steps_ref[lax.axis_index("span")]
    gate = gate_ref[pl.ds(step, 1), :]
    rows = residual_ref.shape[1] // 2
    half = rows // 2
    sums = []
    for y0 in range(2):
        total = pieces_ref[y0].astype(jnp.float32)
        for head in range(1, 4):
            total = total + pieces_ref[2 * head + y0].astype(jnp.float32)
        sums.append(total)
    near, far = sums
    main = jnp.concatenate([near[:half], far[:half], near[half:rows], far[half:rows]])
    rest = HD // 2
    tail = jnp.concatenate([near[rows:, :rest], far[rows:, :rest], near[rows:, rest:], far[rows:, rest:]])
    main = (main * gate[:, :HD]).T
    tail = (tail * gate[:, HD:]).T
    out_ref[:HD, :] = (residual_ref[:HD, :].astype(jnp.float32) + main).astype(jnp.bfloat16)
    out_ref[HD:, :] = (residual_ref[HD:, :].astype(jnp.float32) + tail).astype(jnp.bfloat16)


def shards(q, k, v, block_order, valid_frames, noise_steps, gate_table, out_weight, residual):
    tokens, width = q.shape[1:]
    ny = lax.axis_size(ROW)
    nx = lax.axis_size("span")
    rows = ny * tokens
    swap = [(0, 1), (1, 0)]
    vmem = pl.BlockSpec(memory_space=pltpu.VMEM)
    smem = pl.BlockSpec(memory_space=pltpu.SMEM)
    bf16 = jnp.bfloat16
    params = pltpu.CompilerParams(vmem_limit_bytes=48 * 1024 * 1024)

    def call(kernel, shapes, in_specs, name):
        shapes = [jax.ShapeDtypeStruct(shape, bf16) for shape in shapes]
        return pl.pallas_call(
            kernel,
            out_shape=shapes if len(shapes) > 1 else shapes[0],
            in_specs=in_specs,
            out_specs=[vmem] * len(shapes) if len(shapes) > 1 else vmem,
            compiler_params=params,
            name=name,
        )

    packed = call(pack_kernel, [(ny, 3, tokens, HD)], [vmem] * 3, "pack")(q[0], k[0], v[0])
    with jax.named_scope("exchange_heads"):
        packed = lax.all_to_all(packed, ROW, 0, 0, tiled=True)
    with jax.named_scope("gather_kv"):
        kv = call(keep_kv_kernel, [(2, ny, tokens, HD)], [vmem], "keep_kv")(packed).reshape(2, rows, HD)
        kv_far = lax.ppermute(kv, "zh", swap)
    with jax.named_scope("gather_q"):
        packed, kv = lax.optimization_barrier((packed, kv))
        queries = call(repeat_q_kernel, [(nx, ny, tokens, HD)], [vmem], "repeat_q")(packed)
        queries = lax.all_to_all(queries.reshape(nx, rows, HD), "span", 0, 0, tiled=True)
    with jax.named_scope("gather_kv"):
        near = lax.all_gather(kv, "core", axis=0, tiled=True)
        far = lax.all_gather(kv_far, "core", axis=0, tiled=True)
    with jax.named_scope("fetch_weight"):
        weight, near = lax.optimization_barrier((out_weight.T, near))
        weight_far = lax.ppermute(weight, "y0", swap)
    parts = call(attend_kernel, [(nx, rows + SPACE * -(-rows // HD), HD)], [smem, smem, vmem, vmem, vmem], "attend")(
        block_order, valid_frames, queries, near, far
    )
    with jax.named_scope("return_parts"):
        parts = lax.all_to_all(parts, "span", 0, 0, tiled=True)
        parts, weight_far = lax.optimization_barrier((parts, weight_far))
    near = call(combine_kernel, [(2, rows // 2, HD)], [vmem], "combine")(parts)
    with jax.named_scope("gather_attended"):
        far = lax.ppermute(near, "zh", swap)
        both = call(spread_kernel, [(ny, 2, rows // 2, HD)], [vmem, vmem], "spread")(near, far)
        both = lax.all_to_all(both, ROW, 0, 0, tiled=True)[: width // HD]
        both = lax.all_gather(both, "core", axis=0, tiled=True)
    cols = weight.shape[0]
    pieces = call(project_kernel, [(8, 4 * tokens * cols // HD, HD)], [vmem] * 3, "project")(
        both, weight, weight_far
    )
    with jax.named_scope("sum_heads"):
        pieces = lax.all_to_all(pieces, ("head", "y0"), 0, 0, tiled=True)
    mixed = pl.pallas_call(
        finish_kernel,
        out_shape=jax.ShapeDtypeStruct(residual.shape[:0:-1], bf16),
        in_specs=[smem, vmem, vmem, vmem],
        out_specs=vmem,
        compiler_params=params,
        name="finish",
    )(noise_steps, pieces, gate_table, residual[0].T)
    return mixed.T[None]


def solution(mesh):
    fine = Mesh(mesh.devices.reshape(4, 2, 2, 2, 2, 2, 4), AXES)
    seq = ("zh",) + ROW + ("core",)
    placed = (
        P("span", seq, "head"),
        P("span", seq, "head"),
        P("span", seq, "head"),
        P(),
        P(),
        P(),
        P(None, seq),
        P("head", seq),
        P("span", "head", seq),
    )
    return jax.shard_map(
        shards, mesh=fine, in_specs=placed, out_specs=P("span", "head", seq), check_vma=False
    )
```

```python
import math

import jax
import jax.numpy as jnp
from jax import lax
from jax.experimental import pallas as pl
from jax.experimental.pallas import tpu as pltpu
from jax.sharding import Mesh, PartitionSpec as P

HD = 128
CLOSED = -1e30
LOWEST = -1e20
AXES = ("span", "zh", "y2", "y1", "y0", "core", "head")
ROW = ("y2", "y1", "y0")
FRAME = ("zh", "y2", "y1")
FRAMES = 8


def pack_kernel(q_ref, k_ref, v_ref, out_ref, sems):
    heads = q_ref.shape[1] // HD
    copies = []
    for h in range(heads):
        for i, ref in enumerate((q_ref, k_ref, v_ref)):
            copies.append(
                pltpu.make_async_copy(ref.at[:, h * HD : (h + 1) * HD], out_ref.at[h, i], sems.at[3 * h + i])
            )
    for copy in copies:
        copy.start()
    for h in range(heads, out_ref.shape[0]):
        out_ref[h] = jnp.zeros(out_ref.shape[1:], out_ref.dtype)
    for copy in copies:
        copy.wait()


def unpack_kernel(packed_ref, queries_ref, kv_ref):
    for y in range(packed_ref.shape[0]):
        for i in range(queries_ref.shape[0]):
            queries_ref[i, y] = packed_ref[y, 0]
        for i in range(2):
            kv_ref[i, y] = packed_ref[y, 1 + i]


def attend_kernel(order_ref, valid_ref, q_ref, near_ref, far_ref, out_ref):
    blocks, rows = q_ref.shape[:2]
    zh = lax.axis_index("zh")
    span = lax.axis_index("span")
    keys = jnp.concatenate([ref[i] for ref in (near_ref, far_ref) for i in (0, 2)])
    values = jnp.concatenate([ref[i] for ref in (near_ref, far_ref) for i in (1, 3)])
    place = lax.broadcasted_iota(jnp.int32, (1, 4 * rows), 1)
    inner = place
    for i in range(1, 4):
        inner = jnp.where(place >= i * rows, place - i * rows, inner)
    half = FRAMES // 2
    frame_rows = rows // half
    near_limit = (valid_ref[span] - half * zh) * frame_rows
    far_limit = (valid_ref[span] - half * (1 - zh)) * frame_rows
    limit = jnp.where(place < 2 * rows, near_limit, far_limit)
    bias = jnp.where(inner < limit, 0.0, CLOSED)
    lane = lax.broadcasted_iota(jnp.int32, (rows, HD), 1)
    scale = math.log2(math.e) / HD**0.5
    for block in range(blocks):
        closed = jnp.where(order_ref[span] <= order_ref[block], 0.0, CLOSED)
        s = lax.dot_general(q_ref[block], keys, (((1,), (1,)), ((), ())), preferred_element_type=jnp.float32)
        s = s * scale + (bias + closed)
        top = jnp.maximum(jnp.max(s, axis=1, keepdims=True), LOWEST)
        top = top.astype(jnp.bfloat16).astype(jnp.float32)
        w = jnp.exp2(s - top)
        total = jnp.sum(w, axis=1, keepdims=True)
        acc = jnp.dot(w.astype(jnp.bfloat16), values, preferred_element_type=jnp.float32)
        coarse = total.astype(jnp.bfloat16).astype(jnp.float32)
        stats = jnp.where(lane == 0, top, jnp.where(lane == 1, coarse, total - coarse))
        out_ref[block, :, :HD] = acc.astype(jnp.bfloat16)
        out_ref[block, :, HD:] = stats.astype(jnp.bfloat16)


def combine_kernel(parts_ref, out_ref):
    stats = parts_ref[:, :, HD:].astype(jnp.float32)
    top = stats[:, :, 0:1]
    factor = jnp.exp2(top - jnp.max(top, axis=0, keepdims=True))
    denominator = jnp.sum(factor * (stats[:, :, 1:2] + stats[:, :, 2:3]), axis=0)
    summed = jnp.sum(factor * parts_ref[:, :, :HD].astype(jnp.float32), axis=0)
    done = summed / denominator
    tokens = done.shape[0] // FRAMES
    for y0 in range(2):
        piece = jnp.concatenate([done[(2 * i + y0) * tokens : (2 * i + y0 + 1) * tokens] for i in range(FRAMES // 2)])
        out_ref[y0] = piece.astype(jnp.bfloat16)


def spread_kernel(near_ref, far_ref, out_ref):
    for y in range(out_ref.shape[0]):
        out_ref[y, 0] = near_ref[y % 2]
        out_ref[y, 1] = far_ref[y % 2]


def project_kernel(steps_ref, gates_ref, rows_ref, near_ref, far_ref, out_ref, gate_ref):
    gate_ref[...] = gates_ref[pl.ds(steps_ref[lax.axis_index("span")], 1), :]
    zh = lax.axis_index("zh")
    y0 = lax.axis_index("y0")
    heads = near_ref.shape[1] // HD
    rows = rows_ref.shape[2]
    quarter = rows // 4
    for side in range(2):
        left = [jnp.concatenate([rows_ref[c * heads + h, side] for h in range(heads)], axis=1) for c in range(2)]
        for turn, weight in enumerate((near_ref, far_ref)):
            first, second = [
                lax.dot_general(part, weight[...], (((1,), (1,)), ((), ())), preferred_element_type=jnp.float32)
                for part in left
            ]
            for y2 in range(2):
                a, b = 2 * y2 * quarter, (2 * y2 + 1) * quarter
                piece = jnp.concatenate(
                    [first[a : a + quarter], second[a : a + quarter], first[b : b + quarter], second[b : b + quarter]]
                )
                slot = (2 * (zh ^ side) + y2) * 2 + (y0 ^ turn)
                out_ref[slot, :rows, :] = piece[:, :HD].astype(jnp.bfloat16)
                tail = jnp.concatenate([piece[: rows // 2, HD:], piece[rows // 2 :, HD:]], axis=1)
                out_ref[slot, rows:, :] = tail.astype(jnp.bfloat16)


def finish_kernel(pieces_ref, gate_ref, residual_ref, out_ref):
    gate = gate_ref[...]
    rows = residual_ref.shape[1] // 2
    half = rows // 2
    sums = []
    for y0 in range(2):
        total = pieces_ref[y0].astype(jnp.float32)
        for head in range(1, 4):
            total = total + pieces_ref[2 * head + y0].astype(jnp.float32)
        sums.append(total)
    near, far = sums
    main = jnp.concatenate([near[:half], far[:half], near[half:rows], far[half:rows]])
    rest = HD // 2
    tail = jnp.concatenate([near[rows:, :rest], far[rows:, :rest], near[rows:, rest:], far[rows:, rest:]])
    main = (main * gate[:, :HD]).T
    tail = (tail * gate[:, HD:]).T
    out_ref[:HD, :] = (residual_ref[:HD, :].astype(jnp.float32) + main).astype(jnp.bfloat16)
    out_ref[HD:, :] = (residual_ref[HD:, :].astype(jnp.float32) + tail).astype(jnp.bfloat16)


def shards(q, k, v, block_order, valid_frames, noise_steps, gate_table, out_weight, residual):
    tokens, width = q.shape[1:]
    ny = lax.axis_size(ROW)
    nx = lax.axis_size("span")
    rows = ny * tokens
    swap = [(0, 1), (1, 0)]
    vmem = pl.BlockSpec(memory_space=pltpu.VMEM)
    smem = pl.BlockSpec(memory_space=pltpu.SMEM)
    bf16 = jnp.bfloat16
    params = pltpu.CompilerParams(vmem_limit_bytes=48 * 1024 * 1024)

    def call(kernel, shapes, in_specs, name):
        shapes = [jax.ShapeDtypeStruct(shape, bf16) for shape in shapes]
        return pl.pallas_call(
            kernel,
            out_shape=shapes if len(shapes) > 1 else shapes[0],
            in_specs=in_specs,
            out_specs=[vmem] * len(shapes) if len(shapes) > 1 else vmem,
            compiler_params=params,
            name=name,
        )

    packed = pl.pallas_call(
        pack_kernel,
        out_shape=jax.ShapeDtypeStruct((ny, 3, tokens, HD), bf16),
        in_specs=[pl.BlockSpec(memory_space=pltpu.HBM)] * 3,
        out_specs=vmem,
        scratch_shapes=[pltpu.SemaphoreType.DMA((3 * width // HD,))],
        compiler_params=pltpu.CompilerParams(vmem_limit_bytes=60 * 1024 * 1024),
        name="pack",
    )(q[0], k[0], v[0])
    with jax.named_scope("exchange_heads"):
        packed = lax.all_to_all(packed, ROW, 0, 0, tiled=True)
    queries, kv = call(unpack_kernel, [(nx, ny, tokens, HD), (2, ny, tokens, HD)], [vmem], "unpack")(packed)
    with jax.named_scope("gather_q"):
        queries = lax.all_to_all(queries.reshape(nx, rows, HD), "span", 0, 0, tiled=True)
    with jax.named_scope("gather_kv"):
        kv = kv.reshape(2, rows, HD)
        kv_far = lax.ppermute(kv, "zh", swap)
        near = lax.all_gather(kv, "core", axis=0, tiled=True)
        far = lax.all_gather(kv_far, "core", axis=0, tiled=True)
    with jax.named_scope("fetch_weight"):
        weight, near = lax.optimization_barrier((out_weight.T, near))
        weight_far = lax.ppermute(weight, "y0", swap)
    parts = call(attend_kernel, [(nx, rows, 2 * HD)], [smem, smem, vmem, vmem, vmem], "attend")(
        block_order, valid_frames, queries, near, far
    )
    with jax.named_scope("return_parts"):
        parts = lax.all_to_all(parts, "span", 0, 0, tiled=True)
        parts, weight_far = lax.optimization_barrier((parts, weight_far))
    near = call(combine_kernel, [(2, rows // 2, HD)], [vmem], "combine")(parts)
    with jax.named_scope("gather_attended"):
        far = lax.ppermute(near, "zh", swap)
        both = call(spread_kernel, [(ny, 2, rows // 2, HD)], [vmem, vmem], "spread")(near, far)
        both = lax.all_to_all(both, ROW, 0, 0, tiled=True)[: width // HD]
        both = lax.all_gather(both, "core", axis=0, tiled=True)
    cols = weight.shape[0]
    pieces, gate = pl.pallas_call(
        project_kernel,
        out_shape=(
            jax.ShapeDtypeStruct((8, 4 * tokens * cols // HD, HD), bf16),
            jax.ShapeDtypeStruct((1, cols), jnp.float32),
        ),
        in_specs=[smem] + [vmem] * 4,
        out_specs=(vmem, vmem),
        compiler_params=params,
        name="project",
    )(noise_steps, gate_table, both, weight, weight_far)
    with jax.named_scope("sum_heads"):
        pieces = lax.all_to_all(pieces, ("head", "y0"), 0, 0, tiled=True)
    mixed = pl.pallas_call(
        finish_kernel,
        out_shape=jax.ShapeDtypeStruct(residual.shape[:0:-1], bf16),
        in_specs=[vmem, vmem, vmem],
        out_specs=vmem,
        compiler_params=params,
        name="finish",
    )(pieces, gate, residual[0].T)
    return mixed.T[None]


def solution(mesh):
    fine = Mesh(mesh.devices.reshape(4, 2, 2, 2, 2, 2, 4), AXES)
    seq = ("zh",) + ROW + ("core",)
    placed = (
        P("span", seq, "head"),
        P("span", seq, "head"),
        P("span", seq, "head"),
        P(),
        P(),
        P(),
        P(None, seq),
        P("head", seq),
        P("span", "head", seq),
    )
    return jax.shard_map(
        shards, mesh=fine, in_specs=placed, out_specs=P("span", "head", seq), check_vma=False
    )
```

```python
import functools
import math

import jax
import jax.numpy as jnp
from jax import lax
from jax.experimental import pallas as pl
from jax.experimental.pallas import tpu as pltpu
from jax.sharding import Mesh, PartitionSpec as P

HD = 128
CLOSED = -1e30
LOWEST = -1e20
SPACE = 16
AXES = ("span", "zh", "y2", "y1", "y0", "core", "head")
ROW = ("y2", "y1", "y0")
FRAME = ("zh", "y2", "y1")
FRAMES = 8


def pack_kernel(q_ref, k_ref, v_ref, out_ref, sems):
    heads = q_ref.shape[1] // HD
    copies = []
    for h in range(heads):
        for i, ref in enumerate((q_ref, k_ref, v_ref)):
            copies.append(
                pltpu.make_async_copy(ref.at[:, h * HD : (h + 1) * HD], out_ref.at[h, i], sems.at[3 * h + i])
            )
    for copy in copies:
        copy.start()
    for h in range(heads, out_ref.shape[0]):
        out_ref[h] = jnp.zeros(out_ref.shape[1:], out_ref.dtype)
    for copy in copies:
        copy.wait()


def keep_kv_kernel(packed_ref, kv_ref):
    for y in range(packed_ref.shape[0]):
        for i in range(2):
            kv_ref[i, y] = packed_ref[y, 1 + i]


def repeat_q_kernel(packed_ref, queries_ref):
    for y in range(packed_ref.shape[0]):
        for i in range(queries_ref.shape[0]):
            queries_ref[i, y] = packed_ref[y, 0]


def attend_kernel(order_ref, valid_ref, q_ref, near_ref, far_ref, out_ref):
    blocks, rows = q_ref.shape[:2]
    zh = lax.axis_index("zh")
    span = lax.axis_index("span")
    keys = jnp.concatenate([ref[i] for ref in (near_ref, far_ref) for i in (0, 2)])
    values = jnp.concatenate([ref[i] for ref in (near_ref, far_ref) for i in (1, 3)])
    place = lax.broadcasted_iota(jnp.int32, (1, 4 * rows), 1)
    inner = place
    for i in range(1, 4):
        inner = jnp.where(place >= i * rows, place - i * rows, inner)
    half = FRAMES // 2
    frame_rows = rows // half
    near_limit = (valid_ref[span] - half * zh) * frame_rows
    far_limit = (valid_ref[span] - half * (1 - zh)) * frame_rows
    limit = jnp.where(place < 2 * rows, near_limit, far_limit)
    bias = jnp.where(inner < limit, 0.0, CLOSED)
    lane = lax.broadcasted_iota(jnp.int32, (rows, HD), 1)
    stats = jnp.zeros((rows, HD), jnp.float32)
    scale = math.log2(math.e) / HD**0.5
    for block in range(blocks):
        closed = jnp.where(order_ref[span] <= order_ref[block], 0.0, CLOSED)
        s = lax.dot_general(q_ref[block], keys, (((1,), (1,)), ((), ())), preferred_element_type=jnp.float32)
        s = s * scale + (bias + closed)
        top = jnp.maximum(jnp.max(s, axis=1, keepdims=True), LOWEST)
        top = top.astype(jnp.bfloat16).astype(jnp.float32)
        w = jnp.exp2(s - top)
        total = jnp.sum(w, axis=1, keepdims=True)
        acc = jnp.dot(w.astype(jnp.bfloat16), values, preferred_element_type=jnp.float32)
        out_ref[block, :rows, :] = acc.astype(jnp.bfloat16)
        coarse = total.astype(jnp.bfloat16).astype(jnp.float32)
        stats = jnp.where(lane == SPACE * block, top, stats)
        stats = jnp.where(lane == SPACE * block + 1, coarse, stats)
        stats = jnp.where(lane == SPACE * block + 2, total - coarse, stats)
    places = out_ref.shape[1] - rows
    wide = jnp.concatenate([stats, jnp.zeros((places // SPACE * HD - rows, HD), jnp.float32)]).T
    wide = wide.astype(jnp.bfloat16)
    for block in range(blocks):
        for i in range(places // SPACE):
            piece = wide[SPACE * block : SPACE * (block + 1), i * HD : (i + 1) * HD]
            out_ref[block, rows + SPACE * i : rows + SPACE * (i + 1), :] = piece


def combine_kernel(parts_ref, out_ref):
    blocks = parts_ref.shape[0]
    rows = out_ref.shape[0] * out_ref.shape[1]
    count = (parts_ref.shape[1] - rows) // SPACE
    wide = jnp.concatenate(
        [
            jnp.concatenate([parts_ref[b, rows + SPACE * i : rows + SPACE * (i + 1), :] for i in range(count)], axis=1)
            for b in range(blocks)
        ]
    )
    stats = wide.astype(jnp.float32).T[:rows]
    tops = [stats[:, SPACE * b : SPACE * b + 1] for b in range(blocks)]
    highest = functools.reduce(jnp.maximum, tops)
    denominator, summed = 0.0, 0.0
    for b in range(blocks):
        factor = jnp.exp2(tops[b] - highest)
        place = SPACE * b
        denominator = denominator + factor * (stats[:, place + 1 : place + 2] + stats[:, place + 2 : place + 3])
        summed = summed + factor * parts_ref[b, :rows, :].astype(jnp.float32)
    done = summed / denominator
    tokens = done.shape[0] // FRAMES
    for y0 in range(2):
        piece = jnp.concatenate([done[(2 * i + y0) * tokens : (2 * i + y0 + 1) * tokens] for i in range(FRAMES // 2)])
        out_ref[y0] = piece.astype(jnp.bfloat16)


def spread_kernel(near_ref, far_ref, out_ref):
    for y in range(out_ref.shape[0]):
        out_ref[y, 0] = near_ref[y % 2]
        out_ref[y, 1] = far_ref[y % 2]


def project_kernel(steps_ref, gates_ref, rows_ref, near_ref, far_ref, out_ref, gate_ref):
    gate_ref[...] = gates_ref[pl.ds(steps_ref[lax.axis_index("span")], 1), :]
    zh = lax.axis_index("zh")
    y0 = lax.axis_index("y0")
    heads = near_ref.shape[1] // HD
    rows = rows_ref.shape[2]
    quarter = rows // 4
    for side in range(2):
        left = [jnp.concatenate([rows_ref[c * heads + h, side] for h in range(heads)], axis=1) for c in range(2)]
        for turn, weight in enumerate((near_ref, far_ref)):
            first, second = [
                lax.dot_general(part, weight[...], (((1,), (1,)), ((), ())), preferred_element_type=jnp.float32)
                for part in left
            ]
            for y2 in range(2):
                a, b = 2 * y2 * quarter, (2 * y2 + 1) * quarter
                piece = jnp.concatenate(
                    [first[a : a + quarter], second[a : a + quarter], first[b : b + quarter], second[b : b + quarter]]
                )
                slot = (2 * (zh ^ side) + y2) * 2 + (y0 ^ turn)
                out_ref[slot, :rows, :] = piece[:, :HD].astype(jnp.bfloat16)
                tail = jnp.concatenate([piece[: rows // 2, HD:], piece[rows // 2 :, HD:]], axis=1)
                out_ref[slot, rows:, :] = tail.astype(jnp.bfloat16)


def finish_kernel(pieces_ref, gate_ref, residual_ref, out_ref):
    gate = gate_ref[...]
    rows = residual_ref.shape[1] // 2
    half = rows // 2
    sums = []
    for y0 in range(2):
        total = pieces_ref[y0].astype(jnp.float32)
        for head in range(1, 4):
            total = total + pieces_ref[2 * head + y0].astype(jnp.float32)
        sums.append(total)
    near, far = sums
    main = jnp.concatenate([near[:half], far[:half], near[half:rows], far[half:rows]])
    rest = HD // 2
    tail = jnp.concatenate([near[rows:, :rest], far[rows:, :rest], near[rows:, rest:], far[rows:, rest:]])
    main = (main * gate[:, :HD]).T
    tail = (tail * gate[:, HD:]).T
    out_ref[:HD, :] = (residual_ref[:HD, :].astype(jnp.float32) + main).astype(jnp.bfloat16)
    out_ref[HD:, :] = (residual_ref[HD:, :].astype(jnp.float32) + tail).astype(jnp.bfloat16)


def shards(q, k, v, block_order, valid_frames, noise_steps, gate_table, out_weight, residual):
    tokens, width = q.shape[1:]
    ny = lax.axis_size(ROW)
    nx = lax.axis_size("span")
    rows = ny * tokens
    swap = [(0, 1), (1, 0)]
    vmem = pl.BlockSpec(memory_space=pltpu.VMEM)
    smem = pl.BlockSpec(memory_space=pltpu.SMEM)
    bf16 = jnp.bfloat16
    params = pltpu.CompilerParams(vmem_limit_bytes=48 * 1024 * 1024)

    def call(kernel, shapes, in_specs, name):
        shapes = [jax.ShapeDtypeStruct(shape, bf16) for shape in shapes]
        return pl.pallas_call(
            kernel,
            out_shape=shapes if len(shapes) > 1 else shapes[0],
            in_specs=in_specs,
            out_specs=[vmem] * len(shapes) if len(shapes) > 1 else vmem,
            compiler_params=params,
            name=name,
        )

    packed = pl.pallas_call(
        pack_kernel,
        out_shape=jax.ShapeDtypeStruct((ny, 3, tokens, HD), bf16),
        in_specs=[pl.BlockSpec(memory_space=pltpu.HBM)] * 3,
        out_specs=vmem,
        scratch_shapes=[pltpu.SemaphoreType.DMA((3 * width // HD,))],
        compiler_params=pltpu.CompilerParams(vmem_limit_bytes=60 * 1024 * 1024),
        name="pack",
    )(q[0], k[0], v[0])
    with jax.named_scope("exchange_heads"):
        packed = lax.all_to_all(packed, ROW, 0, 0, tiled=True)
    with jax.named_scope("gather_kv"):
        kv = call(keep_kv_kernel, [(2, ny, tokens, HD)], [vmem], "keep_kv")(packed).reshape(2, rows, HD)
        kv_far = lax.ppermute(kv, "zh", swap)
    with jax.named_scope("gather_q"):
        packed, kv = lax.optimization_barrier((packed, kv))
        queries = call(repeat_q_kernel, [(nx, ny, tokens, HD)], [vmem], "repeat_q")(packed)
        queries = lax.all_to_all(queries.reshape(nx, rows, HD), "span", 0, 0, tiled=True)
    with jax.named_scope("gather_kv"):
        near = lax.all_gather(kv, "core", axis=0, tiled=True)
        far = lax.all_gather(kv_far, "core", axis=0, tiled=True)
    with jax.named_scope("fetch_weight"):
        weight, near = lax.optimization_barrier((out_weight.T, near))
        weight_far = lax.ppermute(weight, "y0", swap)
    parts = call(attend_kernel, [(nx, rows + SPACE * -(-rows // HD), HD)], [smem, smem, vmem, vmem, vmem], "attend")(
        block_order, valid_frames, queries, near, far
    )
    with jax.named_scope("return_parts"):
        parts = lax.all_to_all(parts, "span", 0, 0, tiled=True)
    near = call(combine_kernel, [(2, rows // 2, HD)], [vmem], "combine")(parts)
    with jax.named_scope("gather_attended"):
        near, weight_far = lax.optimization_barrier((near, weight_far))
        far = lax.ppermute(near, "zh", swap)
        both = call(spread_kernel, [(ny, 2, rows // 2, HD)], [vmem, vmem], "spread")(near, far)
        both = lax.all_to_all(both, ROW, 0, 0, tiled=True)[: width // HD]
        both = lax.all_gather(both, "core", axis=0, tiled=True)
    cols = weight.shape[0]
    pieces, gate = pl.pallas_call(
        project_kernel,
        out_shape=(
            jax.ShapeDtypeStruct((8, 4 * tokens * cols // HD, HD), bf16),
            jax.ShapeDtypeStruct((1, cols), jnp.float32),
        ),
        in_specs=[smem] + [vmem] * 4,
        out_specs=(vmem, vmem),
        compiler_params=params,
        name="project",
    )(noise_steps, gate_table, both, weight, weight_far)
    with jax.named_scope("sum_heads"):
        pieces = lax.all_to_all(pieces, ("head", "y0"), 0, 0, tiled=True)
    mixed = pl.pallas_call(
        finish_kernel,
        out_shape=jax.ShapeDtypeStruct(residual.shape[:0:-1], bf16),
        in_specs=[vmem, vmem, vmem],
        out_specs=vmem,
        compiler_params=params,
        name="finish",
    )(pieces, gate, residual[0].T)
    return mixed.T[None]


def solution(mesh):
    fine = Mesh(mesh.devices.reshape(4, 2, 2, 2, 2, 2, 4), AXES)
    seq = ("zh",) + ROW + ("core",)
    placed = (
        P("span", seq, "head"),
        P("span", seq, "head"),
        P("span", seq, "head"),
        P(),
        P(),
        P(),
        P(None, seq),
        P("head", seq),
        P("span", "head", seq),
    )
    return jax.shard_map(
        shards, mesh=fine, in_specs=placed, out_specs=P("span", "head", seq), check_vma=False
    )
```

```python
import math

import jax
import jax.numpy as jnp
from jax import lax
from jax.experimental import pallas as pl
from jax.experimental.pallas import tpu as pltpu
from jax.sharding import Mesh, PartitionSpec as P

HD = 128
CLOSED = -1e30
LOWEST = -1e20
AXES = ("span", "zh", "y2", "y1", "y0", "core", "head")
ROW = ("y2", "y1", "y0")
FRAME = ("zh", "y2", "y1")
FRAMES = 8


def pack_kernel(q_ref, k_ref, v_ref, out_ref, held_ref, sems):
    heads = q_ref.shape[1] // HD
    copies = [
        pltpu.make_async_copy(ref, held_ref.at[i], sems.at[i]) for i, ref in enumerate((q_ref, k_ref, v_ref))
    ]
    for copy in copies:
        copy.start()
    for h in range(heads, out_ref.shape[0]):
        out_ref[h] = jnp.zeros(out_ref.shape[1:], out_ref.dtype)
    for i, copy in enumerate(copies):
        copy.wait()
        for h in range(heads):
            out_ref[h, i] = held_ref[i, :, h * HD : (h + 1) * HD]


def unpack_kernel(packed_ref, queries_ref, kv_ref):
    for y in range(packed_ref.shape[0]):
        for i in range(queries_ref.shape[0]):
            queries_ref[i, y] = packed_ref[y, 0]
        for i in range(2):
            kv_ref[i, y] = packed_ref[y, 1 + i]


def attend_kernel(order_ref, valid_ref, q_ref, near_ref, far_ref, out_ref):
    blocks, rows = q_ref.shape[:2]
    zh = lax.axis_index("zh")
    span = lax.axis_index("span")
    keys = jnp.concatenate([ref[i] for ref in (near_ref, far_ref) for i in (0, 2)])
    values = jnp.concatenate([ref[i] for ref in (near_ref, far_ref) for i in (1, 3)])
    place = lax.broadcasted_iota(jnp.int32, (1, 4 * rows), 1)
    inner = place
    for i in range(1, 4):
        inner = jnp.where(place >= i * rows, place - i * rows, inner)
    half = FRAMES // 2
    frame_rows = rows // half
    near_limit = (valid_ref[span] - half * zh) * frame_rows
    far_limit = (valid_ref[span] - half * (1 - zh)) * frame_rows
    limit = jnp.where(place < 2 * rows, near_limit, far_limit)
    bias = jnp.where(inner < limit, 0.0, CLOSED)
    lane = lax.broadcasted_iota(jnp.int32, (rows, HD), 1)
    scale = math.log2(math.e) / HD**0.5
    for block in range(blocks):
        closed = jnp.where(order_ref[span] <= order_ref[block], 0.0, CLOSED)
        s = lax.dot_general(q_ref[block], keys, (((1,), (1,)), ((), ())), preferred_element_type=jnp.float32)
        s = s * scale + (bias + closed)
        top = jnp.maximum(jnp.max(s, axis=1, keepdims=True), LOWEST)
        top = top.astype(jnp.bfloat16).astype(jnp.float32)
        w = jnp.exp2(s - top)
        total = jnp.sum(w, axis=1, keepdims=True)
        acc = jnp.dot(w.astype(jnp.bfloat16), values, preferred_element_type=jnp.float32)
        coarse = total.astype(jnp.bfloat16).astype(jnp.float32)
        stats = jnp.where(lane == 0, top, jnp.where(lane == 1, coarse, total - coarse))
        out_ref[block, :, :HD] = acc.astype(jnp.bfloat16)
        out_ref[block, :, HD:] = stats.astype(jnp.bfloat16)


def combine_kernel(parts_ref, out_ref):
    stats = parts_ref[:, :, HD:].astype(jnp.float32)
    top = stats[:, :, 0:1]
    factor = jnp.exp2(top - jnp.max(top, axis=0, keepdims=True))
    denominator = jnp.sum(factor * (stats[:, :, 1:2] + stats[:, :, 2:3]), axis=0)
    summed = jnp.sum(factor * parts_ref[:, :, :HD].astype(jnp.float32), axis=0)
    done = summed / denominator
    tokens = done.shape[0] // FRAMES
    for y0 in range(2):
        piece = jnp.concatenate([done[(2 * i + y0) * tokens : (2 * i + y0 + 1) * tokens] for i in range(FRAMES // 2)])
        out_ref[y0] = piece.astype(jnp.bfloat16)


def spread_kernel(near_ref, far_ref, out_ref):
    for y in range(out_ref.shape[0]):
        out_ref[y, 0] = near_ref[y % 2]
        out_ref[y, 1] = far_ref[y % 2]


def project_kernel(steps_ref, gates_ref, rows_ref, near_ref, far_ref, out_ref, gate_ref):
    gate_ref[...] = gates_ref[pl.ds(steps_ref[lax.axis_index("span")], 1), :]
    zh = lax.axis_index("zh")
    y0 = lax.axis_index("y0")
    heads = near_ref.shape[1] // HD
    rows = rows_ref.shape[2]
    quarter = rows // 4
    for side in range(2):
        left = [jnp.concatenate([rows_ref[c * heads + h, side] for h in range(heads)], axis=1) for c in range(2)]
        for turn, weight in enumerate((near_ref, far_ref)):
            first, second = [
                lax.dot_general(part, weight[...], (((1,), (1,)), ((), ())), preferred_element_type=jnp.float32)
                for part in left
            ]
            for y2 in range(2):
                a, b = 2 * y2 * quarter, (2 * y2 + 1) * quarter
                piece = jnp.concatenate(
                    [first[a : a + quarter], second[a : a + quarter], first[b : b + quarter], second[b : b + quarter]]
                )
                slot = (2 * (zh ^ side) + y2) * 2 + (y0 ^ turn)
                out_ref[slot, :rows, :] = piece[:, :HD].astype(jnp.bfloat16)
                tail = jnp.concatenate([piece[: rows // 2, HD:], piece[rows // 2 :, HD:]], axis=1)
                out_ref[slot, rows:, :] = tail.astype(jnp.bfloat16)


def finish_kernel(pieces_ref, gate_ref, residual_ref, out_ref):
    gate = gate_ref[...]
    rows = residual_ref.shape[1] // 2
    half = rows // 2
    sums = []
    for y0 in range(2):
        total = pieces_ref[y0].astype(jnp.float32)
        for head in range(1, 4):
            total = total + pieces_ref[2 * head + y0].astype(jnp.float32)
        sums.append(total)
    near, far = sums
    main = jnp.concatenate([near[:half], far[:half], near[half:rows], far[half:rows]])
    rest = HD // 2
    tail = jnp.concatenate([near[rows:, :rest], far[rows:, :rest], near[rows:, rest:], far[rows:, rest:]])
    main = (main * gate[:, :HD]).T
    tail = (tail * gate[:, HD:]).T
    out_ref[:HD, :] = (residual_ref[:HD, :].astype(jnp.float32) + main).astype(jnp.bfloat16)
    out_ref[HD:, :] = (residual_ref[HD:, :].astype(jnp.float32) + tail).astype(jnp.bfloat16)


def shards(q, k, v, block_order, valid_frames, noise_steps, gate_table, out_weight, residual):
    tokens, width = q.shape[1:]
    ny = lax.axis_size(ROW)
    nx = lax.axis_size("span")
    rows = ny * tokens
    swap = [(0, 1), (1, 0)]
    vmem = pl.BlockSpec(memory_space=pltpu.VMEM)
    smem = pl.BlockSpec(memory_space=pltpu.SMEM)
    bf16 = jnp.bfloat16
    params = pltpu.CompilerParams(vmem_limit_bytes=48 * 1024 * 1024)

    def call(kernel, shapes, in_specs, name):
        shapes = [jax.ShapeDtypeStruct(shape, bf16) for shape in shapes]
        return pl.pallas_call(
            kernel,
            out_shape=shapes if len(shapes) > 1 else shapes[0],
            in_specs=in_specs,
            out_specs=[vmem] * len(shapes) if len(shapes) > 1 else vmem,
            compiler_params=params,
            name=name,
        )

    packed = pl.pallas_call(
        pack_kernel,
        out_shape=jax.ShapeDtypeStruct((ny, 3, tokens, HD), bf16),
        in_specs=[pl.BlockSpec(memory_space=pltpu.HBM)] * 3,
        out_specs=vmem,
        scratch_shapes=[pltpu.VMEM((3, tokens, width), bf16), pltpu.SemaphoreType.DMA((3,))],
        compiler_params=pltpu.CompilerParams(vmem_limit_bytes=60 * 1024 * 1024),
        name="pack",
    )(q[0], k[0], v[0])
    with jax.named_scope("exchange_heads"):
        packed = lax.all_to_all(packed, ROW, 0, 0, tiled=True)
    queries, kv = call(unpack_kernel, [(nx, ny, tokens, HD), (2, ny, tokens, HD)], [vmem], "unpack")(packed)
    with jax.named_scope("gather_q"):
        queries = lax.all_to_all(queries.reshape(nx, rows, HD), "span", 0, 0, tiled=True)
    with jax.named_scope("gather_kv"):
        kv = kv.reshape(2, rows, HD)
        kv_far = lax.ppermute(kv, "zh", swap)
        near = lax.all_gather(kv, "core", axis=0, tiled=True)
        far = lax.all_gather(kv_far, "core", axis=0, tiled=True)
    with jax.named_scope("fetch_weight"):
        weight, near = lax.optimization_barrier((out_weight.T, near))
        weight_far = lax.ppermute(weight, "y0", swap)
    parts = call(attend_kernel, [(nx, rows, 2 * HD)], [smem, smem, vmem, vmem, vmem], "attend")(
        block_order, valid_frames, queries, near, far
    )
    with jax.named_scope("return_parts"):
        parts = lax.all_to_all(parts, "span", 0, 0, tiled=True)
        parts, weight_far = lax.optimization_barrier((parts, weight_far))
    near = call(combine_kernel, [(2, rows // 2, HD)], [vmem], "combine")(parts)
    with jax.named_scope("gather_attended"):
        far = lax.ppermute(near, "zh", swap)
        both = call(spread_kernel, [(ny, 2, rows // 2, HD)], [vmem, vmem], "spread")(near, far)
        both = lax.all_to_all(both, ROW, 0, 0, tiled=True)[: width // HD]
        both = lax.all_gather(both, "core", axis=0, tiled=True)
    cols = weight.shape[0]
    pieces, gate = pl.pallas_call(
        project_kernel,
        out_shape=(
            jax.ShapeDtypeStruct((8, 4 * tokens * cols // HD, HD), bf16),
            jax.ShapeDtypeStruct((1, cols), jnp.float32),
        ),
        in_specs=[smem] + [vmem] * 4,
        out_specs=(vmem, vmem),
        compiler_params=params,
        name="project",
    )(noise_steps, gate_table, both, weight, weight_far)
    with jax.named_scope("sum_heads"):
        pieces = lax.all_to_all(pieces, ("head", "y0"), 0, 0, tiled=True)
    mixed = pl.pallas_call(
        finish_kernel,
        out_shape=jax.ShapeDtypeStruct(residual.shape[:0:-1], bf16),
        in_specs=[vmem, vmem, vmem],
        out_specs=vmem,
        compiler_params=params,
        name="finish",
    )(pieces, gate, residual[0].T)
    return mixed.T[None]


def solution(mesh):
    fine = Mesh(mesh.devices.reshape(4, 2, 2, 2, 2, 2, 4), AXES)
    seq = ("zh",) + ROW + ("core",)
    placed = (
        P("span", seq, "head"),
        P("span", seq, "head"),
        P("span", seq, "head"),
        P(),
        P(),
        P(),
        P(None, seq),
        P("head", seq),
        P("span", "head", seq),
    )
    return jax.shard_map(
        shards, mesh=fine, in_specs=placed, out_specs=P("span", "head", seq), check_vma=False
    )
```

```python
import math

import jax
import jax.numpy as jnp
from jax import lax
from jax.experimental import pallas as pl
from jax.experimental.pallas import tpu as pltpu
from jax.sharding import Mesh, PartitionSpec as P

HD = 128
CLOSED = -1e30
LOWEST = -1e20
AXES = ("span", "zh", "y2", "y1", "y0", "core", "head")
ROW = ("y2", "y1", "y0")
FRAME = ("zh", "y2", "y1")
FRAMES = 8


def pack_kernel(q_ref, k_ref, v_ref, out_ref, held_ref, sems):
    heads = q_ref.shape[1] // HD
    copies = [
        pltpu.make_async_copy(ref, held_ref.at[i], sems.at[i]) for i, ref in enumerate((q_ref, k_ref, v_ref))
    ]
    for copy in copies:
        copy.start()
    for h in range(heads, out_ref.shape[0]):
        out_ref[h] = jnp.zeros(out_ref.shape[1:], out_ref.dtype)
    for i, copy in enumerate(copies):
        copy.wait()
        for h in range(heads):
            out_ref[h, i] = held_ref[i, :, h * HD : (h + 1) * HD]


def unpack_kernel(packed_ref, queries_ref, kv_ref):
    for y in range(packed_ref.shape[0]):
        for i in range(queries_ref.shape[0]):
            queries_ref[i, y] = packed_ref[y, 0]
        for i in range(2):
            kv_ref[i, y] = packed_ref[y, 1 + i]


def attend_kernel(order_ref, valid_ref, q_ref, near_ref, far_ref, out_ref, held_ref, sems):
    blocks, rows = q_ref.shape[:2]
    zh = lax.axis_index("zh")
    span = lax.axis_index("span")
    keys = jnp.concatenate([ref[i] for ref in (near_ref, far_ref) for i in (0, 2)])
    values = jnp.concatenate([ref[i] for ref in (near_ref, far_ref) for i in (1, 3)])
    place = lax.broadcasted_iota(jnp.int32, (1, 4 * rows), 1)
    inner = place
    for i in range(1, 4):
        inner = jnp.where(place >= i * rows, place - i * rows, inner)
    half = FRAMES // 2
    frame_rows = rows // half
    near_limit = (valid_ref[span] - half * zh) * frame_rows
    far_limit = (valid_ref[span] - half * (1 - zh)) * frame_rows
    limit = jnp.where(place < 2 * rows, near_limit, far_limit)
    bias = jnp.where(inner < limit, 0.0, CLOSED)
    lane = lax.broadcasted_iota(jnp.int32, (rows, HD), 1)
    scale = math.log2(math.e) / HD**0.5
    copies = []
    for block in range(blocks):
        closed = jnp.where(order_ref[span] <= order_ref[block], 0.0, CLOSED)
        s = lax.dot_general(q_ref[block], keys, (((1,), (1,)), ((), ())), preferred_element_type=jnp.float32)
        s = s * scale + (bias + closed)
        top = jnp.maximum(jnp.max(s, axis=1, keepdims=True), LOWEST)
        top = top.astype(jnp.bfloat16).astype(jnp.float32)
        w = jnp.exp2(s - top)
        total = jnp.sum(w, axis=1, keepdims=True)
        acc = jnp.dot(w.astype(jnp.bfloat16), values, preferred_element_type=jnp.float32)
        coarse = total.astype(jnp.bfloat16).astype(jnp.float32)
        stats = jnp.where(lane == 0, top, jnp.where(lane == 1, coarse, total - coarse))
        held_ref[block, :, :HD] = acc.astype(jnp.bfloat16)
        held_ref[block, :, HD:] = stats.astype(jnp.bfloat16)
        copy = pltpu.make_async_copy(held_ref.at[block], out_ref.at[block], sems.at[block])
        copy.start()
        copies.append(copy)
    for copy in copies:
        copy.wait()


def combine_kernel(parts_ref, out_ref):
    stats = parts_ref[:, :, HD:].astype(jnp.float32)
    top = stats[:, :, 0:1]
    factor = jnp.exp2(top - jnp.max(top, axis=0, keepdims=True))
    denominator = jnp.sum(factor * (stats[:, :, 1:2] + stats[:, :, 2:3]), axis=0)
    summed = jnp.sum(factor * parts_ref[:, :, :HD].astype(jnp.float32), axis=0)
    done = summed / denominator
    tokens = done.shape[0] // FRAMES
    for y0 in range(2):
        piece = jnp.concatenate([done[(2 * i + y0) * tokens : (2 * i + y0 + 1) * tokens] for i in range(FRAMES // 2)])
        out_ref[y0] = piece.astype(jnp.bfloat16)


def spread_kernel(near_ref, far_ref, out_ref):
    for y in range(out_ref.shape[0]):
        out_ref[y, 0] = near_ref[y % 2]
        out_ref[y, 1] = far_ref[y % 2]


def project_kernel(steps_ref, gates_ref, rows_ref, near_ref, far_ref, out_ref, gate_ref):
    gate_ref[...] = gates_ref[pl.ds(steps_ref[lax.axis_index("span")], 1), :]
    zh = lax.axis_index("zh")
    y0 = lax.axis_index("y0")
    heads = near_ref.shape[1] // HD
    rows = rows_ref.shape[2]
    quarter = rows // 4
    for side in range(2):
        left = [jnp.concatenate([rows_ref[c * heads + h, side] for h in range(heads)], axis=1) for c in range(2)]
        for turn, weight in enumerate((near_ref, far_ref)):
            first, second = [
                lax.dot_general(part, weight[...], (((1,), (1,)), ((), ())), preferred_element_type=jnp.float32)
                for part in left
            ]
            for y2 in range(2):
                a, b = 2 * y2 * quarter, (2 * y2 + 1) * quarter
                piece = jnp.concatenate(
                    [first[a : a + quarter], second[a : a + quarter], first[b : b + quarter], second[b : b + quarter]]
                )
                slot = (2 * (zh ^ side) + y2) * 2 + (y0 ^ turn)
                out_ref[slot, :rows, :] = piece[:, :HD].astype(jnp.bfloat16)
                tail = jnp.concatenate([piece[: rows // 2, HD:], piece[rows // 2 :, HD:]], axis=1)
                out_ref[slot, rows:, :] = tail.astype(jnp.bfloat16)


def finish_kernel(pieces_ref, gate_ref, residual_ref, out_ref):
    gate = gate_ref[...]
    rows = residual_ref.shape[1] // 2
    half = rows // 2
    sums = []
    for y0 in range(2):
        total = pieces_ref[y0].astype(jnp.float32)
        for head in range(1, 4):
            total = total + pieces_ref[2 * head + y0].astype(jnp.float32)
        sums.append(total)
    near, far = sums
    main = jnp.concatenate([near[:half], far[:half], near[half:rows], far[half:rows]])
    rest = HD // 2
    tail = jnp.concatenate([near[rows:, :rest], far[rows:, :rest], near[rows:, rest:], far[rows:, rest:]])
    main = (main * gate[:, :HD]).T
    tail = (tail * gate[:, HD:]).T
    out_ref[:HD, :] = (residual_ref[:HD, :].astype(jnp.float32) + main).astype(jnp.bfloat16)
    out_ref[HD:, :] = (residual_ref[HD:, :].astype(jnp.float32) + tail).astype(jnp.bfloat16)


def shards(q, k, v, block_order, valid_frames, noise_steps, gate_table, out_weight, residual):
    tokens, width = q.shape[1:]
    ny = lax.axis_size(ROW)
    nx = lax.axis_size("span")
    rows = ny * tokens
    swap = [(0, 1), (1, 0)]
    vmem = pl.BlockSpec(memory_space=pltpu.VMEM)
    smem = pl.BlockSpec(memory_space=pltpu.SMEM)
    bf16 = jnp.bfloat16
    params = pltpu.CompilerParams(vmem_limit_bytes=48 * 1024 * 1024)

    def call(kernel, shapes, in_specs, name):
        shapes = [jax.ShapeDtypeStruct(shape, bf16) for shape in shapes]
        return pl.pallas_call(
            kernel,
            out_shape=shapes if len(shapes) > 1 else shapes[0],
            in_specs=in_specs,
            out_specs=[vmem] * len(shapes) if len(shapes) > 1 else vmem,
            compiler_params=params,
            name=name,
        )

    packed = pl.pallas_call(
        pack_kernel,
        out_shape=jax.ShapeDtypeStruct((ny, 3, tokens, HD), bf16),
        in_specs=[pl.BlockSpec(memory_space=pltpu.HBM)] * 3,
        out_specs=vmem,
        scratch_shapes=[pltpu.VMEM((3, tokens, width), bf16), pltpu.SemaphoreType.DMA((3,))],
        compiler_params=pltpu.CompilerParams(vmem_limit_bytes=60 * 1024 * 1024),
        name="pack",
    )(q[0], k[0], v[0])
    with jax.named_scope("exchange_heads"):
        packed = lax.all_to_all(packed, ROW, 0, 0, tiled=True)
    queries, kv = call(unpack_kernel, [(nx, ny, tokens, HD), (2, ny, tokens, HD)], [vmem], "unpack")(packed)
    with jax.named_scope("gather_q"):
        queries = lax.all_to_all(queries.reshape(nx, rows, HD), "span", 0, 0, tiled=True)
    with jax.named_scope("gather_kv"):
        kv = kv.reshape(2, rows, HD)
        kv_far = lax.ppermute(kv, "zh", swap)
        near = lax.all_gather(kv, "core", axis=0, tiled=True)
        far = lax.all_gather(kv_far, "core", axis=0, tiled=True)
    with jax.named_scope("fetch_weight"):
        weight, near = lax.optimization_barrier((out_weight.T, near))
        weight_far = lax.ppermute(weight, "y0", swap)
    parts = pl.pallas_call(
        attend_kernel,
        out_shape=jax.ShapeDtypeStruct((nx, rows, 2 * HD), bf16),
        in_specs=[smem, smem, vmem, vmem, vmem],
        out_specs=pl.BlockSpec(memory_space=pltpu.HBM),
        scratch_shapes=[pltpu.VMEM((nx, rows, 2 * HD), bf16), pltpu.SemaphoreType.DMA((nx,))],
        compiler_params=params,
        name="attend",
    )(block_order, valid_frames, queries, near, far)
    with jax.named_scope("return_parts"):
        parts = lax.all_to_all(parts, "span", 0, 0, tiled=True)
        parts, weight_far = lax.optimization_barrier((parts, weight_far))
    near = call(combine_kernel, [(2, rows // 2, HD)], [vmem], "combine")(parts)
    with jax.named_scope("gather_attended"):
        far = lax.ppermute(near, "zh", swap)
        both = call(spread_kernel, [(ny, 2, rows // 2, HD)], [vmem, vmem], "spread")(near, far)
        both = lax.all_to_all(both, ROW, 0, 0, tiled=True)[: width // HD]
        both = lax.all_gather(both, "core", axis=0, tiled=True)
    cols = weight.shape[0]
    pieces, gate = pl.pallas_call(
        project_kernel,
        out_shape=(
            jax.ShapeDtypeStruct((8, 4 * tokens * cols // HD, HD), bf16),
            jax.ShapeDtypeStruct((1, cols), jnp.float32),
        ),
        in_specs=[smem] + [vmem] * 4,
        out_specs=(vmem, vmem),
        compiler_params=params,
        name="project",
    )(noise_steps, gate_table, both, weight, weight_far)
    with jax.named_scope("sum_heads"):
        pieces = lax.all_to_all(pieces, ("head", "y0"), 0, 0, tiled=True)
    mixed = pl.pallas_call(
        finish_kernel,
        out_shape=jax.ShapeDtypeStruct(residual.shape[:0:-1], bf16),
        in_specs=[vmem, vmem, vmem],
        out_specs=vmem,
        compiler_params=params,
        name="finish",
    )(pieces, gate, residual[0].T)
    return mixed.T[None]


def solution(mesh):
    fine = Mesh(mesh.devices.reshape(4, 2, 2, 2, 2, 2, 4), AXES)
    seq = ("zh",) + ROW + ("core",)
    placed = (
        P("span", seq, "head"),
        P("span", seq, "head"),
        P("span", seq, "head"),
        P(),
        P(),
        P(),
        P(None, seq),
        P("head", seq),
        P("span", "head", seq),
    )
    return jax.shard_map(
        shards, mesh=fine, in_specs=placed, out_specs=P("span", "head", seq), check_vma=False
    )
```

```python
import math

import jax
import jax.numpy as jnp
from jax import lax
from jax.experimental import pallas as pl
from jax.experimental.pallas import tpu as pltpu
from jax.sharding import Mesh, PartitionSpec as P

HD = 128
CLOSED = -1e30
LOWEST = -1e20
AXES = ("span", "zh", "y2", "y1", "y0", "core", "head")
ROW = ("y2", "y1", "y0")
FRAME = ("zh", "y2", "y1")
FRAMES = 8


def pack_kernel(q_ref, k_ref, v_ref, out_ref, held_ref, sems):
    heads = q_ref.shape[1] // HD
    copies = [
        pltpu.make_async_copy(ref, held_ref.at[i], sems.at[i]) for i, ref in enumerate((q_ref, k_ref, v_ref))
    ]
    for copy in copies:
        copy.start()
    for h in range(heads, out_ref.shape[0]):
        out_ref[h] = jnp.zeros(out_ref.shape[1:], out_ref.dtype)
    for i, copy in enumerate(copies):
        copy.wait()
        for h in range(heads):
            out_ref[h, i] = held_ref[i, :, h * HD : (h + 1) * HD]


def keep_kv_kernel(packed_ref, kv_ref):
    for y in range(packed_ref.shape[0]):
        for i in range(2):
            kv_ref[i, y] = packed_ref[y, 1 + i]


def repeat_q_kernel(packed_ref, queries_ref):
    for y in range(packed_ref.shape[0]):
        for i in range(queries_ref.shape[0]):
            queries_ref[i, y] = packed_ref[y, 0]


def attend_kernel(order_ref, valid_ref, q_ref, near_ref, far_ref, out_ref, held_ref, sems):
    blocks, rows = q_ref.shape[:2]
    zh = lax.axis_index("zh")
    span = lax.axis_index("span")
    keys = jnp.concatenate([ref[i] for ref in (near_ref, far_ref) for i in (0, 2)])
    values = jnp.concatenate([ref[i] for ref in (near_ref, far_ref) for i in (1, 3)])
    place = lax.broadcasted_iota(jnp.int32, (1, 4 * rows), 1)
    inner = place
    for i in range(1, 4):
        inner = jnp.where(place >= i * rows, place - i * rows, inner)
    half = FRAMES // 2
    frame_rows = rows // half
    near_limit = (valid_ref[span] - half * zh) * frame_rows
    far_limit = (valid_ref[span] - half * (1 - zh)) * frame_rows
    limit = jnp.where(place < 2 * rows, near_limit, far_limit)
    bias = jnp.where(inner < limit, 0.0, CLOSED)
    lane = lax.broadcasted_iota(jnp.int32, (rows, HD), 1)
    scale = math.log2(math.e) / HD**0.5
    copies = []
    for block in range(blocks):
        closed = jnp.where(order_ref[span] <= order_ref[block], 0.0, CLOSED)
        s = lax.dot_general(q_ref[block], keys, (((1,), (1,)), ((), ())), preferred_element_type=jnp.float32)
        s = s * scale + (bias + closed)
        top = jnp.maximum(jnp.max(s, axis=1, keepdims=True), LOWEST)
        top = top.astype(jnp.bfloat16).astype(jnp.float32)
        w = jnp.exp2(s - top)
        total = jnp.sum(w, axis=1, keepdims=True)
        acc = jnp.dot(w.astype(jnp.bfloat16), values, preferred_element_type=jnp.float32)
        coarse = total.astype(jnp.bfloat16).astype(jnp.float32)
        stats = jnp.where(lane == 0, top, jnp.where(lane == 1, coarse, total - coarse))
        held_ref[block, :, :HD] = acc.astype(jnp.bfloat16)
        held_ref[block, :, HD:] = stats.astype(jnp.bfloat16)
        copy = pltpu.make_async_copy(held_ref.at[block], out_ref.at[block], sems.at[block])
        copy.start()
        copies.append(copy)
    for copy in copies:
        copy.wait()


def combine_kernel(parts_ref, out_ref):
    stats = parts_ref[:, :, HD:].astype(jnp.float32)
    top = stats[:, :, 0:1]
    factor = jnp.exp2(top - jnp.max(top, axis=0, keepdims=True))
    denominator = jnp.sum(factor * (stats[:, :, 1:2] + stats[:, :, 2:3]), axis=0)
    summed = jnp.sum(factor * parts_ref[:, :, :HD].astype(jnp.float32), axis=0)
    done = summed / denominator
    tokens = done.shape[0] // FRAMES
    for y0 in range(2):
        piece = jnp.concatenate([done[(2 * i + y0) * tokens : (2 * i + y0 + 1) * tokens] for i in range(FRAMES // 2)])
        out_ref[y0] = piece.astype(jnp.bfloat16)


def spread_kernel(near_ref, far_ref, out_ref):
    for y in range(out_ref.shape[0]):
        out_ref[y, 0] = near_ref[y % 2]
        out_ref[y, 1] = far_ref[y % 2]


def project_kernel(steps_ref, gates_ref, rows_ref, near_ref, far_ref, out_ref, gate_ref):
    gate_ref[...] = gates_ref[pl.ds(steps_ref[lax.axis_index("span")], 1), :]
    zh = lax.axis_index("zh")
    y0 = lax.axis_index("y0")
    heads = near_ref.shape[1] // HD
    rows = rows_ref.shape[2]
    quarter = rows // 4
    for side in range(2):
        left = [jnp.concatenate([rows_ref[c * heads + h, side] for h in range(heads)], axis=1) for c in range(2)]
        for turn, weight in enumerate((near_ref, far_ref)):
            first, second = [
                lax.dot_general(part, weight[...], (((1,), (1,)), ((), ())), preferred_element_type=jnp.float32)
                for part in left
            ]
            for y2 in range(2):
                a, b = 2 * y2 * quarter, (2 * y2 + 1) * quarter
                piece = jnp.concatenate(
                    [first[a : a + quarter], second[a : a + quarter], first[b : b + quarter], second[b : b + quarter]]
                )
                slot = (2 * (zh ^ side) + y2) * 2 + (y0 ^ turn)
                out_ref[slot, :rows, :] = piece[:, :HD].astype(jnp.bfloat16)
                tail = jnp.concatenate([piece[: rows // 2, HD:], piece[rows // 2 :, HD:]], axis=1)
                out_ref[slot, rows:, :] = tail.astype(jnp.bfloat16)


def finish_kernel(pieces_ref, gate_ref, residual_ref, out_ref):
    gate = gate_ref[...]
    rows = residual_ref.shape[1] // 2
    half = rows // 2
    sums = []
    for y0 in range(2):
        total = pieces_ref[y0].astype(jnp.float32)
        for head in range(1, 4):
            total = total + pieces_ref[2 * head + y0].astype(jnp.float32)
        sums.append(total)
    near, far = sums
    main = jnp.concatenate([near[:half], far[:half], near[half:rows], far[half:rows]])
    rest = HD // 2
    tail = jnp.concatenate([near[rows:, :rest], far[rows:, :rest], near[rows:, rest:], far[rows:, rest:]])
    main = (main * gate[:, :HD]).T
    tail = (tail * gate[:, HD:]).T
    out_ref[:HD, :] = (residual_ref[:HD, :].astype(jnp.float32) + main).astype(jnp.bfloat16)
    out_ref[HD:, :] = (residual_ref[HD:, :].astype(jnp.float32) + tail).astype(jnp.bfloat16)


def shards(q, k, v, block_order, valid_frames, noise_steps, gate_table, out_weight, residual):
    tokens, width = q.shape[1:]
    ny = lax.axis_size(ROW)
    nx = lax.axis_size("span")
    rows = ny * tokens
    swap = [(0, 1), (1, 0)]
    vmem = pl.BlockSpec(memory_space=pltpu.VMEM)
    smem = pl.BlockSpec(memory_space=pltpu.SMEM)
    bf16 = jnp.bfloat16
    params = pltpu.CompilerParams(vmem_limit_bytes=48 * 1024 * 1024)

    def call(kernel, shapes, in_specs, name):
        shapes = [jax.ShapeDtypeStruct(shape, bf16) for shape in shapes]
        return pl.pallas_call(
            kernel,
            out_shape=shapes if len(shapes) > 1 else shapes[0],
            in_specs=in_specs,
            out_specs=[vmem] * len(shapes) if len(shapes) > 1 else vmem,
            compiler_params=params,
            name=name,
        )

    packed = pl.pallas_call(
        pack_kernel,
        out_shape=jax.ShapeDtypeStruct((ny, 3, tokens, HD), bf16),
        in_specs=[pl.BlockSpec(memory_space=pltpu.HBM)] * 3,
        out_specs=vmem,
        scratch_shapes=[pltpu.VMEM((3, tokens, width), bf16), pltpu.SemaphoreType.DMA((3,))],
        compiler_params=pltpu.CompilerParams(vmem_limit_bytes=60 * 1024 * 1024),
        name="pack",
    )(q[0], k[0], v[0])
    with jax.named_scope("exchange_heads"):
        packed = lax.all_to_all(packed, ROW, 0, 0, tiled=True)
    with jax.named_scope("gather_kv"):
        kv = call(keep_kv_kernel, [(2, ny, tokens, HD)], [vmem], "keep_kv")(packed).reshape(2, rows, HD)
        kv_far = lax.ppermute(kv, "zh", swap)
    with jax.named_scope("gather_q"):
        packed, kv = lax.optimization_barrier((packed, kv))
        queries = call(repeat_q_kernel, [(nx, ny, tokens, HD)], [vmem], "repeat_q")(packed)
        queries = lax.all_to_all(queries.reshape(nx, rows, HD), "span", 0, 0, tiled=True)
    with jax.named_scope("gather_kv"):
        near = lax.all_gather(kv, "core", axis=0, tiled=True)
        far = lax.all_gather(kv_far, "core", axis=0, tiled=True)
    with jax.named_scope("fetch_weight"):
        weight, near = lax.optimization_barrier((out_weight.T, near))
        weight_far = lax.ppermute(weight, "y0", swap)
    parts = pl.pallas_call(
        attend_kernel,
        out_shape=jax.ShapeDtypeStruct((nx, rows, 2 * HD), bf16),
        in_specs=[smem, smem, vmem, vmem, vmem],
        out_specs=pl.BlockSpec(memory_space=pltpu.HBM),
        scratch_shapes=[pltpu.VMEM((nx, rows, 2 * HD), bf16), pltpu.SemaphoreType.DMA((nx,))],
        compiler_params=params,
        name="attend",
    )(block_order, valid_frames, queries, near, far)
    with jax.named_scope("return_parts"):
        parts = lax.all_to_all(parts, "span", 0, 0, tiled=True)
        parts, weight_far = lax.optimization_barrier((parts, weight_far))
    near = call(combine_kernel, [(2, rows // 2, HD)], [vmem], "combine")(parts)
    with jax.named_scope("gather_attended"):
        far = lax.ppermute(near, "zh", swap)
        both = call(spread_kernel, [(ny, 2, rows // 2, HD)], [vmem, vmem], "spread")(near, far)
        both = lax.all_to_all(both, ROW, 0, 0, tiled=True)[: width // HD]
        both = lax.all_gather(both, "core", axis=0, tiled=True)
    cols = weight.shape[0]
    pieces, gate = pl.pallas_call(
        project_kernel,
        out_shape=(
            jax.ShapeDtypeStruct((8, 4 * tokens * cols // HD, HD), bf16),
            jax.ShapeDtypeStruct((1, cols), jnp.float32),
        ),
        in_specs=[smem] + [vmem] * 4,
        out_specs=(vmem, vmem),
        compiler_params=params,
        name="project",
    )(noise_steps, gate_table, both, weight, weight_far)
    with jax.named_scope("sum_heads"):
        pieces = lax.all_to_all(pieces, ("head", "y0"), 0, 0, tiled=True)
    mixed = pl.pallas_call(
        finish_kernel,
        out_shape=jax.ShapeDtypeStruct(residual.shape[:0:-1], bf16),
        in_specs=[vmem, vmem, vmem],
        out_specs=vmem,
        compiler_params=params,
        name="finish",
    )(pieces, gate, residual[0].T)
    return mixed.T[None]


def solution(mesh):
    fine = Mesh(mesh.devices.reshape(4, 2, 2, 2, 2, 2, 4), AXES)
    seq = ("zh",) + ROW + ("core",)
    placed = (
        P("span", seq, "head"),
        P("span", seq, "head"),
        P("span", seq, "head"),
        P(),
        P(),
        P(),
        P(None, seq),
        P("head", seq),
        P("span", "head", seq),
    )
    return jax.shard_map(
        shards, mesh=fine, in_specs=placed, out_specs=P("span", "head", seq), check_vma=False
    )
```
